256 devices in a mesh: row: 16 (over y, x), proto: 16 (over z, core).
Axes of the slice: x: 4, y: 4, z: 8, core: 2. Of those that a mesh axis runs over, the one named last changes fastest.
Arguments:
- embeddings: bfloat16 [32768, 1024], P('row'), may hold values from -24 to 24, as said below
- prototypes: bfloat16 [16384, 1024], P('proto', 'row'), may hold values from -6 to 6
- block_mask: int32 [256, 128], P('row', 'proto'), may hold values from 0 to 1, as said below
Outputs:
- targets: bfloat16 [32768, 1024], P('row', 'proto')
- row_potential: float32 [32768], P('row')
- column_potential: float32 [16384], P('proto')
The draws below stay inside these ranges and needn't reach their ends.
Inputs may be any that keep to these rules, and one draw needn't show every extreme that they name: `block_mask`: every row tile and every prototype tile has at least one candidate tile. `embeddings`: some rows copy a scaled prototype.
All inputs are finite; a program needn't handle non-finite values.
Results may differ from the reference program's by a relative error of at most 0.02.
Values may be sent and summed in bfloat16 or wider, within the bound.
A program may use at most 64 MiB of HBM per device.

```python
import math
import jax
import jax.numpy as jnp
from jax import lax

D = 1024
TILE = 128
ITERS = 3
R_DEV = 2048
K_DEV = 1024
ROWS = 32768
PROTOS = 16384
ROW_BLOCKS = 256
PROTO_BLOCKS = 128
N_PROTO = 16


def layout(key):
    row_perm = jax.random.permutation(jax.random.fold_in(key, 11), ROW_BLOCKS)
    proto_perm = jax.random.permutation(jax.random.fold_in(key, 12), PROTO_BLOCKS)
    return (row_perm, proto_perm)


def drawn(key):
    row_perm, proto_perm = layout(key)
    modulus = min(ROW_BLOCKS, PROTO_BLOCKS)
    chosen = jnp.arange(0, ROW_BLOCKS, 8, dtype=jnp.int32)
    inverse = jnp.argsort(proto_perm)
    proto_block = inverse[row_perm[chosen] % modulus].astype(jnp.int32)
    rows_at = chosen * TILE + 3
    protos_at = proto_block * TILE + 5
    strength = 3.5 + 1.75 * (proto_block % 3).astype(jnp.float32)
    return (rows_at, protos_at, strength)


def proto_base(key):
    inner = jax.random.fold_in(key, 21)
    rows_at, protos_at, strength = drawn(key)
    base = jnp.clip(jax.random.normal(inner, (PROTOS, D), jnp.float32), -6.0, 6.0)
    shrink = 1.0 / (16.0 * strength)
    noise = 0.02 * jax.random.normal(jax.random.fold_in(key, 22), (protos_at.shape[0], D), jnp.float32)
    base = base.at[protos_at + 1].set((1.0 - shrink)[:, None] * base[protos_at] + noise)
    return jnp.clip(base, -6.0, 6.0)


def draw_prototypes(key, part):
    return proto_base(key).astype(jnp.bfloat16)


def draw_embeddings(key, part):
    values = jnp.clip(jax.random.normal(jax.random.fold_in(key, 31), (ROWS, D), jnp.float32), -6.0, 6.0)
    base = proto_base(key).astype(jnp.bfloat16).astype(jnp.float32)
    rows_at, protos_at, strength = drawn(key)
    factor = strength * (8.0 / math.sqrt(D))
    values = values.at[rows_at].set(factor[:, None] * base[protos_at])
    return jnp.clip(values, -24.0, 24.0).astype(jnp.bfloat16)


def draw_block_mask(key, part):
    row_perm, proto_perm = layout(key)
    modulus = min(ROW_BLOCKS, PROTO_BLOCKS)
    sure = row_perm[:, None] % modulus == proto_perm[None, :] % modulus
    level = 100 + 200 * jnp.arange(ROW_BLOCKS, dtype=jnp.int32) // ROW_BLOCKS
    rolled = jax.random.randint(jax.random.fold_in(key, 13), (ROW_BLOCKS, PROTO_BLOCKS), 0, 1000)
    return jnp.where(sure | (rolled < level[:, None]), 1, 0).astype(jnp.int32)


def setup_inputs(seed: int = 0) -> dict:
    keys = jax.random.split(jax.random.key(seed), 4)
    return {
        "embeddings": draw_embeddings(jax.random.fold_in(keys[3], 71), 0),
        "prototypes": draw_prototypes(jax.random.fold_in(keys[3], 71), 0),
        "block_mask": draw_block_mask(jax.random.fold_in(keys[3], 71), 0),
    }


NEGATIVE = -1e+30

def expand_mask(mask_rows):
    allowed = mask_rows == 1
    return jnp.repeat(jnp.repeat(allowed, TILE, axis=0), TILE, axis=1)

def reference(embeddings, prototypes, block_mask):
    scale = 4.0 / math.sqrt(D)
    protos_wide = prototypes.astype(jnp.float32)
    log_column = math.log(ROWS / PROTOS)
    blocks = jnp.arange(ROWS // R_DEV, dtype=jnp.int32)

    def similar_block(index):
        rows_part = lax.dynamic_slice_in_dim(embeddings, index * R_DEV, R_DEV, 0).astype(jnp.float32)
        mask_part = lax.dynamic_slice_in_dim(block_mask, index * (R_DEV // TILE), R_DEV // TILE, 0)
        similar = jnp.dot(rows_part, protos_wide.T, precision=lax.Precision.HIGHEST) * scale
        return (similar, expand_mask(mask_part))
    column_potential = jnp.zeros((PROTOS,), jnp.float32)
    row_potential = jnp.zeros((ROWS,), jnp.float32)
    for sweep in range(ITERS):

        def one_block(carry, index):
            column_peak, column_total = carry
            similar, allowed = similar_block(index)
            shifted = similar + column_potential[None, :]
            peak = lax.optimization_barrier(jnp.max(jnp.where(allowed, shifted, NEGATIVE), axis=1))
            total = lax.optimization_barrier(jnp.sum(jnp.where(allowed, jnp.exp(shifted - peak[:, None]), 0.0), axis=1))
            row_block = -(peak + jnp.log(total))
            lifted = similar + row_block[:, None]
            block_peak = lax.optimization_barrier(jnp.max(jnp.where(allowed, lifted, NEGATIVE), axis=0))
            new_peak = jnp.maximum(column_peak, block_peak)
            new_total = column_total * jnp.exp(column_peak - new_peak) + lax.optimization_barrier(jnp.sum(jnp.where(allowed, jnp.exp(lifted - new_peak[None, :]), 0.0), axis=0))
            return ((new_peak, new_total), row_block)
        start = (jnp.full((PROTOS,), NEGATIVE, jnp.float32), jnp.zeros((PROTOS,), jnp.float32))
        (column_peak, column_total), row_blocks = lax.scan(one_block, start, blocks)
        row_potential = row_blocks.reshape(ROWS)
        column_potential = log_column - (column_peak + jnp.log(column_total))

    def final_block(index):
        similar, allowed = similar_block(index)
        row_part = lax.dynamic_slice_in_dim(row_potential, index * R_DEV, R_DEV, 0)
        plan = jnp.where(allowed, jnp.exp(similar + row_part[:, None] + column_potential[None, :]), 0.0).astype(jnp.bfloat16)
        plan_wide = plan.reshape(R_DEV, N_PROTO, K_DEV).astype(jnp.float32)
        protos_split = protos_wide.reshape(N_PROTO, K_DEV, D)
        partial_value = jnp.einsum('rnk,nkd->nrd', plan_wide, protos_split, precision=lax.Precision.HIGHEST).astype(jnp.bfloat16)
        return lax.optimization_barrier(jnp.sum(partial_value.astype(jnp.float32), axis=0)).astype(jnp.bfloat16)
    targets = lax.map(final_block, blocks).reshape(ROWS, D)
    return (targets, row_potential, column_potential)
```

```python
import functools
import math

import jax
import jax.numpy as jnp
from jax import lax
from jax.experimental import pallas as pl
from jax.experimental.pallas import tpu as pltpu
from jax.sharding import PartitionSpec as P

ITERS = 3
TILE = 128
NEGATIVE = -1e30
LOWEST = -1e38
LOG2E = 1.4426950408889634
LN2 = 0.6931471805599453
MESH = pl.DeviceIdType.MESH


def tree_reduce(op, parts):
    while len(parts) > 1:
        pairs = [op(parts[i], parts[i + 1]) for i in range(0, len(parts) - 1, 2)]
        parts = pairs + ([parts[-1]] if len(parts) % 2 else [])
    return parts[0]


def kernel(
    cfg,
    own_ref,
    emb_hbm,
    mask_ref,
    out_ref,
    row_out,
    col_out,
    emb,
    feat,
    sim,
    wide,
    row_send,
    row_recv,
    col_send,
    col_recv,
    part,
    sib_recv,
    tx,
    rx,
    emb_sem,
    gs_sem,
    gr_sem,
    rs_sem,
    rr_sem,
    cs_sem,
    cr_sem,
    ss_sem,
    sr_sem,
    ts_sem,
    tr_sem,
):
    side, n_row, n_proto, log_column = cfg
    n_z = n_proto // 2
    slab, protos = own_ref.shape
    share = out_ref.shape[0]
    depth = feat.shape[0]
    rows = sim.shape[0]
    row_tiles, col_tiles = rows // TILE, protos // TILE
    scale = 4.0 / math.sqrt(depth) * LOG2E

    r = lax.axis_index("row")
    p = lax.axis_index("proto")
    y, x = r // side, lax.rem(r, side)
    z, c = p // 2, lax.rem(p, 2)

    def row_of(dy, dx):
        return lax.rem(y + dy + 2 * side, side) * side + lax.rem(x + dx + 2 * side, side)

    emb_copy = pltpu.make_async_copy(emb_hbm, emb, emb_sem)
    emb_copy.start()

    barrier = pltpu.get_barrier_semaphore()
    for d in range(1, n_row):
        pl.semaphore_signal(
            barrier, inc=1, device_id=(lax.rem(r + d, n_row), p), device_id_type=MESH
        )
    for d in range(1, n_proto):
        pl.semaphore_signal(
            barrier, inc=1, device_id=(r, lax.rem(p + d, n_proto)), device_id_type=MESH
        )
    pl.semaphore_wait(barrier, n_row + n_proto - 2)

    half, quarter = slab // 2, slab // 4

    def shift(tree, df, ds):
        return (ds, df) if tree == 0 else (df, ds)

    def piece(tree, df, ds, which, ref=None):
        start = tree * half + (quarter if which == "hi" else 0)
        size = half if which == "all" else quarter
        if ref is not None:
            return ref.at[pl.ds(start, size), :]
        return feat.at[pl.ds(pl.multiple_of(row_of(*shift(tree, df, ds)) * slab + start, quarter), size), :]

    moves = {}

    def gather_copy(tree, key, src_at, move, which, from_own):
        slot = moves.setdefault((tree, key), len([k for k in moves if k[0] == tree]))
        block = piece(tree, *src_at, which)
        src = piece(tree, 0, 0, which, own_ref) if from_own else block
        return pltpu.make_async_remote_copy(
            src_ref=src,
            dst_ref=block,
            send_sem=gs_sem.at[tree, slot],
            recv_sem=gr_sem.at[tree, slot],
            device_id=(row_of(*shift(tree, *move)), p),
            device_id_type=MESH,
        )

    sent = []

    def push(tree, key, src_at, move, which, from_own=False):
        copy = gather_copy(tree, key, src_at, move, which, from_own)
        copy.start()
        sent.append(copy)

    if n_row > 1:
        trees = (0, 1)
        for t in trees:
            push(t, "f+", (0, 0), (1, 0), "all", True)
            push(t, "f-", (0, 0), (-1, 0), "all", True)
        for t in trees:
            push(t, "s+0", (0, 0), (0, 1), "all", True)
            push(t, "s-0", (0, 0), (0, -1), "all", True)

    feat[pl.ds(pl.multiple_of(r * slab, slab), slab), :] = own_ref[...]

    if n_row > 1:

        def across(t, df):
            push(t, "s+%d" % df, (df, 0), (0, 1), "all")
            push(t, "s-%d" % df, (df, 0), (0, -1), "all")

        def relay(t, df):
            arrive(t, "s+%d" % df, (df, -1), (0, 1))
            push(t, "t+%d" % df, (df, -1), (0, 1), "lo")
            arrive(t, "s-%d" % df, (df, 1), (0, -1))
            push(t, "t-%d" % df, (df, 1), (0, -1), "hi")

        def arrive(t, key, at, move, which="all"):
            slot = moves[(t, key)]
            block = piece(t, *at, which)
            pltpu.make_async_remote_copy(
                src_ref=block,
                dst_ref=block,
                send_sem=gs_sem.at[t, slot],
                recv_sem=gr_sem.at[t, slot],
                device_id=(row_of(*shift(t, *move)), p),
                device_id_type=MESH,
            ).wait_recv()

        for t in trees:
            arrive(t, "f+", (-1, 0), (1, 0))
            push(t, "g+", (-1, 0), (1, 0), "lo")
            arrive(t, "f-", (1, 0), (-1, 0))
            push(t, "g-", (1, 0), (-1, 0), "hi")
        for t in trees:
            across(t, -1)
            across(t, 1)
        for t in trees:
            relay(t, 0)
        for t in trees:
            arrive(t, "g+", (2, 0), (1, 0), "lo")
            arrive(t, "g-", (2, 0), (-1, 0), "hi")
            across(t, 2)
        for t in trees:
            relay(t, -1)
            relay(t, 1)
        for t in trees:
            relay(t, 2)
        for t in trees:
            for df in (0, -1, 1, 2):
                arrive(t, "t+%d" % df, (df, 2), (0, 1), "lo")
                arrive(t, "t-%d" % df, (df, 2), (0, -1), "hi")

    emb_copy.wait()

    mm, mn = min(512, rows), min(256, protos)

    def score_block(step, carry):
        i, j = step // (protos // mn), lax.rem(step, protos // mn)
        row0 = pl.multiple_of(i * mm, mm)
        col0 = pl.multiple_of(j * mn, mn)
        acc = jnp.dot(
            emb[pl.ds(row0, mm), :], feat[:, pl.ds(col0, mn)], preferred_element_type=jnp.float32
        )
        for a in range(mm // TILE):
            for b in range(mn // TILE):
                allowed = mask_ref[i * (mm // TILE) + a, j * (mn // TILE) + b] == 1
                bias = jnp.where(allowed, 0.0, NEGATIVE)
                sim[
                    pl.ds(pl.multiple_of(row0 + a * TILE, TILE), TILE),
                    pl.ds(pl.multiple_of(col0 + b * TILE, TILE), TILE),
                ] = acc[a * TILE : (a + 1) * TILE, b * TILE : (b + 1) * TILE] * scale + bias
        return carry

    lax.fori_loop(0, (rows // mm) * (protos // mn), score_block, 0)

    group = 16

    def row_partial(shifts):
        def block(step, carry):
            base = pl.multiple_of(step * group, group)
            vals = []
            for j in range(col_tiles):
                v = sim[pl.ds(base, group), j * TILE : (j + 1) * TILE]
                if shifts is not None:
                    v = v + shifts[j : j + 1, :]
                vals.append(v)
            peak = tree_reduce(jnp.maximum, vals)
            total = tree_reduce(jnp.add, [jnp.exp2(v - peak) for v in vals])
            wide[pl.ds(base, group), :] = peak + jnp.log2(total)
            return carry

        lax.fori_loop(0, rows // group, block, 0, unroll=2)

    def row_finish(k):
        def block(i, carry):
            t = jnp.transpose(wide[pl.ds(pl.multiple_of(i * TILE, TILE), TILE), :])
            peak = jnp.max(t, axis=0, keepdims=True)
            total = jnp.sum(jnp.exp2(t - peak), axis=0, keepdims=True)
            row_send[k, pl.ds(i, 1), :] = peak + jnp.log2(total)
            return carry

        lax.fori_loop(0, row_tiles, block, 0, unroll=4)

    def exchange(send, recv, send_sem, recv_sem, k, n, target):
        for d in range(1, n):
            pltpu.make_async_remote_copy(
                src_ref=send.at[k],
                dst_ref=recv.at[k, d - 1],
                send_sem=send_sem.at[k],
                recv_sem=recv_sem.at[k],
                device_id=target(d),
                device_id_type=MESH,
            ).start()
        if n > 1:
            pltpu.make_async_remote_copy(
                src_ref=recv.at[k],
                dst_ref=recv.at[k],
                send_sem=send_sem.at[k],
                recv_sem=recv_sem.at[k],
                device_id=target(1),
                device_id_type=MESH,
            ).wait()
        parts = [send[k]] + [recv[k, d - 1] for d in range(1, n)]
        peak = tree_reduce(jnp.maximum, parts)
        total = tree_reduce(jnp.add, [jnp.exp2(v - peak) for v in parts])
        return peak + jnp.log2(total)

    def spread_rows():
        def block(i, carry):
            u = jnp.broadcast_to(row_out[pl.ds(i, 1), :], (TILE, TILE))
            wide[pl.ds(pl.multiple_of(i * TILE, TILE), TILE), :] = jnp.transpose(u)
            return carry

        lax.fori_loop(0, row_tiles, block, 0, unroll=4)

    def column_partial(k):
        def block(i, carry):
            base = pl.multiple_of(i * TILE, TILE)
            out = []
            for j in range(col_tiles):
                top, total = carry[j]
                v = sim[pl.ds(base, TILE), j * TILE : (j + 1) * TILE] + wide[pl.ds(base, TILE), :]
                v = v.reshape(TILE // 8, 8, TILE)
                new = jnp.maximum(top, tree_reduce(jnp.maximum, [v[g] for g in range(TILE // 8)]))
                add = tree_reduce(jnp.add, [jnp.exp2(v[g] - new) for g in range(TILE // 8)])
                out.append((new, total * jnp.exp2(top - new) + add))
            return tuple(out)

        start = tuple(
            (jnp.full((8, TILE), LOWEST, jnp.float32), jnp.zeros((8, TILE), jnp.float32))
            for _ in range(col_tiles)
        )
        done = lax.fori_loop(0, row_tiles, block, start)
        for j in range(col_tiles):
            level = done[j][0] + jnp.log2(done[j][1])
            peak = jnp.max(level, axis=0, keepdims=True)
            total = jnp.sum(jnp.exp2(level - peak), axis=0, keepdims=True)
            col_send[k, j : j + 1, :] = peak + jnp.log2(total)

    shifts = None
    for k in range(ITERS):
        row_partial(shifts)
        row_finish(k)
        row_out[...] = -exchange(
            row_send, row_recv, rs_sem, rr_sem, k, n_proto, lambda d: (r, lax.rem(p + d, n_proto))
        )
        spread_rows()
        column_partial(k)
        shifts = log_column - exchange(
            col_send, col_recv, cs_sem, cr_sem, k, n_row, lambda d: (lax.rem(r + d, n_row), p)
        )

    col_out[...] = shifts * LN2

    plan = emb

    def plan_block(step, carry):
        base = pl.multiple_of(step * group, group)
        u = wide[pl.ds(base, group), :]
        for j in range(col_tiles):
            v = sim[pl.ds(base, group), j * TILE : (j + 1) * TILE] + (u + shifts[j : j + 1, :])
            plan[pl.ds(base, group), j * TILE : (j + 1) * TILE] = jnp.exp2(v).astype(jnp.bfloat16)
        return carry

    lax.fori_loop(0, rows // group, plan_block, 0, unroll=2)
    row_out[...] = row_out[...] * LN2

    width = rows // 2
    tn = min(256, rows)

    def product(t):
        feat0 = pl.multiple_of(lax.rem(z + t, n_z) * 2 * share, 2 * share)

        def block(n, carry):
            row0 = pl.multiple_of(n * tn, tn)
            part[t, :, pl.ds(row0, tn)] = lax.dot_general(
                feat[pl.ds(feat0, 2 * share), :],
                plan[pl.ds(row0, tn), :],
                (((1,), (1,)), ((), ())),
                preferred_element_type=jnp.float32,
            ).astype(jnp.bfloat16)
            return carry

        lax.fori_loop(0, rows // tn, block, 0)

    def sibling_copy(t):
        other = 1 - c
        return pltpu.make_async_remote_copy(
            src_ref=part.at[t, pl.ds(pl.multiple_of(other * share, share), share), :],
            dst_ref=sib_recv.at[t],
            send_sem=ss_sem.at[t],
            recv_sem=sr_sem.at[t],
            device_id=(r, z * 2 + other),
            device_id_type=MESH,
        )

    def chip_sum(t, h):
        mine = part[t, pl.ds(pl.multiple_of(c * share, share), share), h * width : (h + 1) * width]
        theirs = sib_recv[t, :, h * width : (h + 1) * width]
        return mine.astype(jnp.float32) + theirs.astype(jnp.float32)

    def chain_copy(way, d, h):
        step = 1 if way == 0 else n_z - 1
        return pltpu.make_async_remote_copy(
            src_ref=tx.at[way, d - 1, h],
            dst_ref=rx.at[way, d - 1, h],
            send_sem=ts_sem.at[way, d - 1, h],
            recv_sem=tr_sem.at[way, d - 1, h],
            device_id=(r, lax.rem(z + step, n_z) * 2 + c),
            device_id_type=MESH,
        )

    far = n_z // 2
    flying = []

    def forward(way, d, h):
        t = d if way == 0 else n_z - d
        value = chip_sum(t, h)
        if d < far and (d + 1 < far or h == way):
            chain_copy(way, d + 1, h).wait_recv()
            value = value + rx[way, d, h].astype(jnp.float32)
        tx[way, d - 1, h] = value.astype(jnp.bfloat16)
        copy = chain_copy(way, d, h)
        copy.start()
        flying.append(copy)

    def ready(t):
        product(t)
        copy = sibling_copy(t)
        copy.start()
        return copy

    waiting = {}
    order = [far] + [t for d in range(far - 1, 0, -1) for t in (d, n_z - d)] + [0] if far else [0]
    for t in order[:3]:
        waiting[t] = ready(t)
    if far:
        waiting[far].wait()
        forward(0, far, 0)
        forward(1, far, 1)
    done = 3
    for d in range(far - 1, 0, -1):
        for t in (d, n_z - d):
            waiting[t].wait()
        forward(0, d, 1)
        forward(1, d, 0)
        for t in order[done : done + 2]:
            waiting[t] = ready(t)
        done += 2
        forward(0, d, 0)
        forward(1, d, 1)
    for t in order[done:]:
        waiting[t] = ready(t)
    waiting[0].wait()
    for h in (1, 0):
        value = chip_sum(0, h)
        for way in (0, 1):
            if far > 1 or (far == 1 and h == way):
                chain_copy(way, 1, h).wait_recv()
                value = value + rx[way, 0, h].astype(jnp.float32)
        out_ref[:, h * width : (h + 1) * width] = value.astype(jnp.bfloat16)

    for copy in sent + flying:
        copy.wait_send()


def solution(mesh):
    n_row, n_proto = mesh.shape["row"], mesh.shape["proto"]
    side = math.isqrt(n_row)
    n_z = n_proto // 2
    far = max(n_z // 2, 1)

    def shards(embeddings, prototypes, block_mask):
        rows, depth = embeddings.shape
        protos, slab = prototypes.shape
        share = depth // n_proto
        row_tiles, col_tiles = rows // TILE, protos // TILE
        log_column = math.log2((rows * n_row) / (protos * n_proto))
        f32, bf16 = jnp.float32, jnp.bfloat16
        dma = pltpu.SemaphoreType.DMA
        peers_r, peers_p = max(n_row - 1, 1), max(n_proto - 1, 1)
        vmem = pl.BlockSpec(memory_space=pltpu.VMEM)
        targets, row_potential, column_potential = pl.pallas_call(
            functools.partial(kernel, (side, n_row, n_proto, log_column)),
            out_shape=(
                jax.ShapeDtypeStruct((share, rows), bf16),
                jax.ShapeDtypeStruct((row_tiles, TILE), f32),
                jax.ShapeDtypeStruct((col_tiles, TILE), f32),
            ),
            in_specs=[
                vmem,
                pl.BlockSpec(memory_space=pl.ANY),
                pl.BlockSpec(memory_space=pltpu.SMEM),
            ],
            out_specs=(vmem, vmem, vmem),
            scratch_shapes=[
                pltpu.VMEM((rows, depth), bf16),
                pltpu.VMEM((depth, protos), bf16),
                pltpu.VMEM((rows, protos), f32),
                pltpu.VMEM((rows, TILE), f32),
                pltpu.VMEM((ITERS, row_tiles, TILE), f32),
                pltpu.VMEM((ITERS, peers_p, row_tiles, TILE), f32),
                pltpu.VMEM((ITERS, col_tiles, TILE), f32),
                pltpu.VMEM((ITERS, peers_r, col_tiles, TILE), f32),
                pltpu.VMEM((n_z, 2 * share, rows), bf16),
                pltpu.VMEM((n_z, share, rows), bf16),
                pltpu.VMEM((2, far, 2, share, rows // 2), bf16),
                pltpu.VMEM((2, far, 2, share, rows // 2), bf16),
                dma(()),
                dma((2, 20)),
                dma((2, 20)),
                dma((ITERS,)),
                dma((ITERS,)),
                dma((ITERS,)),
                dma((ITERS,)),
                dma((n_z,)),
                dma((n_z,)),
                dma((2, far, 2)),
                dma((2, far, 2)),
            ],
            compiler_params=pltpu.CompilerParams(
                collective_id=0, has_side_effects=True, vmem_limit_bytes=56 * 1024 * 1024
            ),
        )(prototypes.T, embeddings, block_mask)
        return (
            targets.T,
            row_potential.reshape(rows),
            column_potential.reshape(protos),
        )

    return jax.shard_map(
        shards,
        mesh=mesh,
        in_specs=(P("row", None), P("proto", "row"), P("row", "proto")),
        out_specs=(P("row", "proto"), P("row"), P("proto")),
        check_vma=False,
    )
```

```python
import functools
import math

import jax
import jax.numpy as jnp
from jax import lax
from jax.experimental import pallas as pl
from jax.experimental.pallas import tpu as pltpu
from jax.sharding import PartitionSpec as P

ITERS = 3
TILE = 128
NEGATIVE = -1e30
LOWEST = -1e38
LOG2E = 1.4426950408889634
LN2 = 0.6931471805599453
SPLIT = 4
MESH = pl.DeviceIdType.MESH


def tree_reduce(op, parts):
    while len(parts) > 1:
        pairs = [op(parts[i], parts[i + 1]) for i in range(0, len(parts) - 1, 2)]
        parts = pairs + ([parts[-1]] if len(parts) % 2 else [])
    return parts[0]


def kernel(
    cfg,
    own_ref,
    emb_hbm,
    mask_ref,
    out_ref,
    row_out,
    col_out,
    emb,
    feat,
    feat_t,
    sim,
    wide,
    row_send,
    row_recv,
    col_send,
    col_recv,
    part,
    sib_recv,
    tx,
    rx,
    emb_sem,
    gs_sem,
    gr_sem,
    rs_sem,
    rr_sem,
    cs_sem,
    cr_sem,
    ss_sem,
    sr_sem,
    ts_sem,
    tr_sem,
):
    side, n_row, n_proto, log_column = cfg
    n_z = n_proto // 2
    slab, protos = own_ref.shape
    share = out_ref.shape[0]
    depth = feat.shape[0]
    rows = sim.shape[0]
    row_tiles, col_tiles = rows // TILE, protos // TILE
    scale = 4.0 / math.sqrt(depth) * LOG2E

    r = lax.axis_index("row")
    p = lax.axis_index("proto")
    y, x = r // side, lax.rem(r, side)
    z, c = p // 2, lax.rem(p, 2)

    def row_of(dy, dx):
        return lax.rem(y + dy + 2 * side, side) * side + lax.rem(x + dx + 2 * side, side)

    emb_copy = pltpu.make_async_copy(emb_hbm, emb, emb_sem)
    emb_copy.start()

    barrier = pltpu.get_barrier_semaphore()
    for d in range(1, n_row):
        pl.semaphore_signal(
            barrier, inc=1, device_id=(lax.rem(r + d, n_row), p), device_id_type=MESH
        )
    for d in range(1, n_proto):
        pl.semaphore_signal(
            barrier, inc=1, device_id=(r, lax.rem(p + d, n_proto)), device_id_type=MESH
        )
    pl.semaphore_wait(barrier, n_row + n_proto - 2)

    half, quarter = slab // 2, slab // 4

    def shift(tree, df, ds):
        return (ds, df) if tree == 0 else (df, ds)

    def piece(tree, df, ds, which, ref=None):
        start = tree * half + (quarter if which == "hi" else 0)
        size = half if which == "all" else quarter
        if ref is not None:
            return ref.at[pl.ds(start, size), :]
        return feat.at[pl.ds(pl.multiple_of(row_of(*shift(tree, df, ds)) * slab + start, quarter), size), :]

    moves = {}

    def gather_copy(tree, key, src_at, move, which, from_own):
        slot = moves.setdefault((tree, key), len([k for k in moves if k[0] == tree]))
        block = piece(tree, *src_at, which)
        src = piece(tree, 0, 0, which, own_ref) if from_own else block
        return pltpu.make_async_remote_copy(
            src_ref=src,
            dst_ref=block,
            send_sem=gs_sem.at[tree, slot],
            recv_sem=gr_sem.at[tree, slot],
            device_id=(row_of(*shift(tree, *move)), p),
            device_id_type=MESH,
        )

    sent = []

    def push(tree, key, src_at, move, which, from_own=False):
        copy = gather_copy(tree, key, src_at, move, which, from_own)
        copy.start()
        sent.append(copy)

    if n_row > 1:
        trees = (0, 1)
        for t in trees:
            push(t, "f+", (0, 0), (1, 0), "all", True)
            push(t, "f-", (0, 0), (-1, 0), "all", True)
        for t in trees:
            push(t, "s+0", (0, 0), (0, 1), "all", True)
            push(t, "s-0", (0, 0), (0, -1), "all", True)

    feat[pl.ds(pl.multiple_of(r * slab, slab), slab), :] = own_ref[...]

    if n_row > 1:

        def across(t, df):
            push(t, "s+%d" % df, (df, 0), (0, 1), "all")
            push(t, "s-%d" % df, (df, 0), (0, -1), "all")

        def relay(t, df):
            arrive(t, "s+%d" % df, (df, -1), (0, 1))
            push(t, "t+%d" % df, (df, -1), (0, 1), "lo")
            arrive(t, "s-%d" % df, (df, 1), (0, -1))
            push(t, "t-%d" % df, (df, 1), (0, -1), "hi")

        def arrive(t, key, at, move, which="all"):
            slot = moves[(t, key)]
            block = piece(t, *at, which)
            pltpu.make_async_remote_copy(
                src_ref=block,
                dst_ref=block,
                send_sem=gs_sem.at[t, slot],
                recv_sem=gr_sem.at[t, slot],
                device_id=(row_of(*shift(t, *move)), p),
                device_id_type=MESH,
            ).wait_recv()

        for t in trees:
            arrive(t, "f+", (-1, 0), (1, 0))
            push(t, "g+", (-1, 0), (1, 0), "lo")
            arrive(t, "f-", (1, 0), (-1, 0))
            push(t, "g-", (1, 0), (-1, 0), "hi")
        for t in trees:
            across(t, -1)
            across(t, 1)
        for t in trees:
            relay(t, 0)
        for t in trees:
            arrive(t, "g+", (2, 0), (1, 0), "lo")
            arrive(t, "g-", (2, 0), (-1, 0), "hi")
            across(t, 2)
        for t in trees:
            relay(t, -1)
            relay(t, 1)
        for t in trees:
            relay(t, 2)
        for t in trees:
            for df in (0, -1, 1, 2):
                arrive(t, "t+%d" % df, (df, 2), (0, 1), "lo")
                arrive(t, "t-%d" % df, (df, 2), (0, -1), "hi")

    emb_copy.wait()

    mm = min(512, rows)

    def lane_lse(vals):
        peak = tree_reduce(jnp.maximum, vals)
        return peak + jnp.log2(tree_reduce(jnp.add, [jnp.exp2(v - peak) for v in vals]))

    def score_block(i, carry):
        row0 = pl.multiple_of(i * mm, mm)
        acc = jnp.dot(emb[pl.ds(row0, mm), :], feat[...], preferred_element_type=jnp.float32)
        for a in range(mm // TILE):
            bias = [
                jnp.where(mask_ref[j, i * (mm // TILE) + a] == 1, 0.0, NEGATIVE)
                for j in range(col_tiles)
            ]
            for g in range(a * TILE, (a + 1) * TILE, 8):
                vals = [
                    acc[g : g + 8, j * TILE : (j + 1) * TILE] * scale + bias[j]
                    for j in range(col_tiles)
                ]
                for j in range(col_tiles):
                    sim[pl.ds(row0 + g, 8), j * TILE : (j + 1) * TILE] = vals[j]
                wide[pl.ds(row0 + g, 8), :] = lane_lse(vals)
        return carry

    lax.fori_loop(0, rows // mm, score_block, 0)

    group = 64

    def lanes(shifts):
        return [jnp.broadcast_to(shifts[j : j + 1, :], (8, TILE)) for j in range(col_tiles)]

    def row_partial(shifts):
        def block(step, carry):
            base = pl.multiple_of(step * group, group)
            for g in range(0, group, 8):
                wide[pl.ds(base + g, 8), :] = lane_lse(
                    [sim[pl.ds(base + g, 8), j * TILE : (j + 1) * TILE] + shifts[j] for j in range(col_tiles)]
                )
            return carry

        lax.fori_loop(0, rows // group, block, 0)

    def row_finish(k):
        def block(i, carry):
            t = jnp.transpose(wide[pl.ds(pl.multiple_of(i * TILE, TILE), TILE), :])
            peak = jnp.max(t, axis=0, keepdims=True)
            total = jnp.sum(jnp.exp2(t - peak), axis=0, keepdims=True)
            row_send[k, pl.ds(i, 1), :] = peak + jnp.log2(total)
            return carry

        lax.fori_loop(0, row_tiles, block, 0, unroll=4)

    def exchange_start(send, recv, send_sem, recv_sem, k, n, target, near):
        for d in sorted(range(1, n), key=lambda d: (-near(d), d)):
            pltpu.make_async_remote_copy(
                src_ref=send.at[k],
                dst_ref=recv.at[k, d - 1],
                send_sem=send_sem.at[k],
                recv_sem=recv_sem.at[k],
                device_id=target(d),
                device_id_type=MESH,
            ).start()

    def exchange_end(send, recv, send_sem, recv_sem, k, n, target):
        if n > 1:
            pltpu.make_async_remote_copy(
                src_ref=recv.at[k],
                dst_ref=recv.at[k],
                send_sem=send_sem.at[k],
                recv_sem=recv_sem.at[k],
                device_id=target(1),
                device_id_type=MESH,
            ).wait()
        parts = [send[k]] + [recv[k, d - 1] for d in range(1, n)]
        peak = tree_reduce(jnp.maximum, parts)
        total = tree_reduce(jnp.add, [jnp.exp2(v - peak) for v in parts])
        return peak + jnp.log2(total)

    def spread_rows():
        def block(i, carry):
            u = jnp.broadcast_to(row_out[pl.ds(i, 1), :], (TILE, TILE))
            wide[pl.ds(pl.multiple_of(i * TILE, TILE), TILE), :] = jnp.transpose(u)
            return carry

        lax.fori_loop(0, row_tiles, block, 0, unroll=4)

    def column_partial(k):
        def block(i, carry):
            base = pl.multiple_of(i * TILE, TILE)
            out = []
            for j in range(col_tiles):
                top, total = carry[j]
                v = sim[pl.ds(base, TILE), j * TILE : (j + 1) * TILE] + wide[pl.ds(base, TILE), :]
                v = v.reshape(TILE // 8, 8, TILE)
                new = jnp.maximum(top, tree_reduce(jnp.maximum, [v[g] for g in range(TILE // 8)]))
                add = tree_reduce(jnp.add, [jnp.exp2(v[g] - new) for g in range(TILE // 8)])
                out.append((new, total * jnp.exp2(top - new) + add))
            return tuple(out)

        start = tuple(
            (jnp.full((8, TILE), LOWEST, jnp.float32), jnp.zeros((8, TILE), jnp.float32))
            for _ in range(col_tiles)
        )
        done = lax.fori_loop(0, row_tiles, block, start)
        for j in range(col_tiles):
            level = done[j][0] + jnp.log2(done[j][1])
            peak = jnp.max(level, axis=0, keepdims=True)
            total = jnp.sum(jnp.exp2(level - peak), axis=0, keepdims=True)
            col_send[k, j : j + 1, :] = peak + jnp.log2(total)

    def proto_peer(d):
        return (r, lax.rem(p + d, n_proto))

    def row_peer(d):
        return (lax.rem(r + d, n_row), p)

    def wrap(d, n):
        return min(d, n - d)

    shifts = None
    for k in range(ITERS):
        if k > 0:
            row_partial(lanes(shifts))
        row_finish(k)
        exchange_start(
            row_send, row_recv, rs_sem, rr_sem, k, n_proto, proto_peer, lambda d: wrap(d, n_proto)
        )
        if k == 0:
            for i in range(0, protos, TILE):
                for j in range(0, depth, TILE):
                    feat_t[i : i + TILE, j : j + TILE] = jnp.transpose(feat[j : j + TILE, i : i + TILE])
        row_out[...] = -exchange_end(row_send, row_recv, rs_sem, rr_sem, k, n_proto, proto_peer)
        spread_rows()
        column_partial(k)
        exchange_start(
            col_send,
            col_recv,
            cs_sem,
            cr_sem,
            k,
            n_row,
            row_peer,
            lambda d: wrap(d // side, side) + wrap(d % side, side),
        )
        shifts = log_column - exchange_end(col_send, col_recv, cs_sem, cr_sem, k, n_row, row_peer)

    col_out[...] = shifts * LN2
    shifts = lanes(shifts)

    plan = emb
    far = n_z // 2
    order = [far] + [t for d in range(far - 1, 0, -1) for t in (d, n_z - d)] + [0] if far else [0]
    pairs = [order[i : i + 2] for i in range(0, len(order), 2)]
    width = rows // SPLIT
    mp = rows // 2
    sent_sibling = []

    def plan_block(base):
        for g in range(0, mp, 16):
            shift = [wide[pl.ds(base + g + e, 8), :] for e in (0, 8)]
            for j in range(col_tiles):
                v = [
                    jnp.exp2(sim[pl.ds(base + g + e, 8), j * TILE : (j + 1) * TILE] + (shift[e // 8] + shifts[j]))
                    for e in (0, 8)
                ]
                plan[pl.ds(base + g, 16), j * TILE : (j + 1) * TILE] = jnp.concatenate(v, axis=0).astype(
                    jnp.bfloat16
                )

    def product(ts, base):
        weights = [
            feat_t[:, pl.ds(pl.multiple_of(lax.rem(z + t, n_z) * 2 * share, 2 * share), 2 * share)] for t in ts
        ]
        acc = jnp.dot(
            plan[pl.ds(base, mp), :],
            jnp.concatenate(weights, axis=1) if len(ts) > 1 else weights[0],
            preferred_element_type=jnp.float32,
        )
        for i, t in enumerate(ts):
            part[t, :, pl.ds(base, mp)] = jnp.transpose(acc[:, i * 2 * share : (i + 1) * 2 * share]).astype(
                jnp.bfloat16
            )

    def sibling_copy(t, h):
        other = 1 - c
        return pltpu.make_async_remote_copy(
            src_ref=part.at[t, pl.ds(pl.multiple_of(other * share, share), share), h * width : (h + 1) * width],
            dst_ref=sib_recv.at[t, h],
            send_sem=ss_sem.at[t, h],
            recv_sem=sr_sem.at[t, h],
            device_id=(r, z * 2 + other),
            device_id_type=MESH,
        )

    def to_sibling(ts, hs):
        for t in ts:
            for h in hs:
                copy = sibling_copy(t, h)
                copy.start()
                sent_sibling.append(copy)

    def chip_sum(t, h):
        sibling_copy(t, h).wait_recv()
        mine = part[t, pl.ds(pl.multiple_of(c * share, share), share), h * width : (h + 1) * width]
        return mine.astype(jnp.float32) + sib_recv[t, h].astype(jnp.float32)

    def chain_copy(way, d, h):
        step = 1 if way == 0 else n_z - 1
        return pltpu.make_async_remote_copy(
            src_ref=tx.at[way, d - 1, h],
            dst_ref=rx.at[way, d - 1, h],
            send_sem=ts_sem.at[way, d - 1, h],
            recv_sem=tr_sem.at[way, d - 1, h],
            device_id=(r, lax.rem(z + step, n_z) * 2 + c),
            device_id_type=MESH,
        )

    flying = []
    lower, upper = list(range(SPLIT // 2)), list(range(SPLIT // 2, SPLIT))
    whole_way = (lower, upper)
    rest = (upper, lower)

    def forward(way, d, hs):
        t = d if way == 0 else n_z - d
        for h in hs:
            value = chip_sum(t, h)
            if d < far and (d + 1 < far or h in whole_way[way]):
                chain_copy(way, d + 1, h).wait_recv()
                value = value + rx[way, d, h].astype(jnp.float32)
            tx[way, d - 1, h] = value.astype(jnp.bfloat16)
            copy = chain_copy(way, d, h)
            copy.start()
            flying.append(copy)

    def later_pair(n):
        if n < len(pairs):

            def block(i, carry):
                product(pairs[n], pl.multiple_of(i * mp, mp))
                return carry

            lax.fori_loop(0, 2, block, 0)
            to_sibling(pairs[n], lower + upper)

    for i, hs in enumerate((lower, upper)):
        plan_block(i * mp)
        product(pairs[0], i * mp)
        to_sibling(pairs[0], hs)
    if far:
        forward(0, far, lower)
        forward(1, far, upper)
    if far > 1:
        forward(0, far - 1, upper)
    later_pair(1)
    if far > 1:
        forward(1, far - 1, lower)
    later_pair(2)
    if far > 1:
        forward(0, far - 1, lower)
        forward(1, far - 1, upper)
    later_pair(3)
    for d in range(far - 2, 0, -1):
        for h, g in zip(upper + lower, lower + upper):
            forward(0, d, [h])
            forward(1, d, [g])
    for h in upper + lower:
        value = chip_sum(0, h)
        for way in (0, 1):
            if far > 1 or (far == 1 and h in whole_way[way]):
                chain_copy(way, 1, h).wait_recv()
                value = value + rx[way, 0, h].astype(jnp.float32)
        out_ref[:, h * width : (h + 1) * width] = value.astype(jnp.bfloat16)
    row_out[...] = row_out[...] * LN2

    for copy in sent + sent_sibling + flying:
        copy.wait_send()


def hand_over(a, b, c, a_out, b_out, c_out, sem):
    copies = [
        pltpu.make_async_copy(src, dst, sem.at[i])
        for i, (src, dst) in enumerate(((a, a_out), (b, b_out), (c, c_out)))
    ]
    for copy in copies:
        copy.start()
    for copy in copies:
        copy.wait()


def solution(mesh):
    n_row, n_proto = mesh.shape["row"], mesh.shape["proto"]
    side = math.isqrt(n_row)
    n_z = n_proto // 2
    far = max(n_z // 2, 1)

    def shards(embeddings, prototypes, block_mask):
        rows, depth = embeddings.shape
        protos, slab = prototypes.shape
        share = depth // n_proto
        row_tiles, col_tiles = rows // TILE, protos // TILE
        log_column = math.log2((rows * n_row) / (protos * n_proto))
        f32, bf16 = jnp.float32, jnp.bfloat16
        dma = pltpu.SemaphoreType.DMA
        peers_r, peers_p = max(n_row - 1, 1), max(n_proto - 1, 1)
        vmem = pl.BlockSpec(memory_space=pltpu.VMEM)
        shapes = (
            jax.ShapeDtypeStruct((share, rows), bf16),
            jax.ShapeDtypeStruct((row_tiles, TILE), f32),
            jax.ShapeDtypeStruct((col_tiles, TILE), f32),
        )
        results = pl.pallas_call(
            functools.partial(kernel, (side, n_row, n_proto, log_column)),
            out_shape=shapes,
            in_specs=[
                vmem,
                pl.BlockSpec(memory_space=pl.ANY),
                pl.BlockSpec(memory_space=pltpu.SMEM),
            ],
            out_specs=(vmem, vmem, vmem),
            scratch_shapes=[
                pltpu.VMEM((rows, depth), bf16),
                pltpu.VMEM((depth, protos), bf16),
                pltpu.VMEM((protos, depth), bf16),
                pltpu.VMEM((rows, protos), f32),
                pltpu.VMEM((rows, TILE), f32),
                pltpu.VMEM((ITERS, row_tiles, TILE), f32),
                pltpu.VMEM((ITERS, peers_p, row_tiles, TILE), f32),
                pltpu.VMEM((ITERS, col_tiles, TILE), f32),
                pltpu.VMEM((ITERS, peers_r, col_tiles, TILE), f32),
                pltpu.VMEM((n_z, 2 * share, rows), bf16),
                pltpu.VMEM((n_z, SPLIT, share, rows // SPLIT), bf16),
                pltpu.VMEM((2, far, SPLIT, share, rows // SPLIT), bf16),
                pltpu.VMEM((2, far, SPLIT, share, rows // SPLIT), bf16),
                dma(()),
                dma((2, 20)),
                dma((2, 20)),
                dma((ITERS,)),
                dma((ITERS,)),
                dma((ITERS,)),
                dma((ITERS,)),
                dma((n_z, SPLIT)),
                dma((n_z, SPLIT)),
                dma((2, far, SPLIT)),
                dma((2, far, SPLIT)),
            ],
            compiler_params=pltpu.CompilerParams(
                collective_id=0, has_side_effects=True, vmem_limit_bytes=56 * 1024 * 1024
            ),
        )(prototypes.T, embeddings, block_mask.T)
        anywhere = pl.BlockSpec(memory_space=pl.ANY)
        targets, row_potential, column_potential = pl.pallas_call(
            hand_over,
            out_shape=shapes,
            in_specs=[anywhere] * 3,
            out_specs=(anywhere,) * 3,
            scratch_shapes=[dma((3,))],
        )(*results)
        return (
            targets.T,
            row_potential.reshape(rows),
            column_potential.reshape(protos),
        )

    return jax.shard_map(
        shards,
        mesh=mesh,
        in_specs=(P("row", None), P("proto", "row"), P("row", "proto")),
        out_specs=(P("row", "proto"), P("row"), P("proto")),
        check_vma=False,
    )
```

```python
import functools
import math

import jax
import jax.numpy as jnp
from jax import lax
from jax.experimental import pallas as pl
from jax.experimental.pallas import tpu as pltpu
from jax.sharding import PartitionSpec as P

ITERS = 3
TILE = 128
NEGATIVE = -1e30
LOWEST = -1e38
LOG2E = 1.4426950408889634
LN2 = 0.6931471805599453
SPLIT = 4
PARTS = 2
MESH = pl.DeviceIdType.MESH


def tree_reduce(op, parts):
    while len(parts) > 1:
        pairs = [op(parts[i], parts[i + 1]) for i in range(0, len(parts) - 1, 2)]
        parts = pairs + ([parts[-1]] if len(parts) % 2 else [])
    return parts[0]


def kernel(
    cfg,
    own_ref,
    emb_hbm,
    mask_ref,
    out_ref,
    row_out,
    col_out,
    emb,
    feat,
    feat_t,
    sim,
    wide,
    row_send,
    row_recv,
    col_send,
    col_recv,
    part,
    sib_recv,
    tx,
    rx,
    emb_sem,
    gs_sem,
    gr_sem,
    rs_sem,
    rr_sem,
    cs_sem,
    cr_sem,
    ss_sem,
    sr_sem,
    ts_sem,
    tr_sem,
):
    side, n_row, n_proto, log_column = cfg
    n_z = n_proto // 2
    slab, protos = own_ref.shape
    share = out_ref.shape[0]
    depth = feat.shape[0]
    rows = sim.shape[0]
    row_tiles, col_tiles = rows // TILE, protos // TILE
    scale = 4.0 / math.sqrt(depth) * LOG2E

    r = lax.axis_index("row")
    p = lax.axis_index("proto")
    y, x = r // side, lax.rem(r, side)
    z, c = p // 2, lax.rem(p, 2)

    def row_of(dy, dx):
        return lax.rem(y + dy + 2 * side, side) * side + lax.rem(x + dx + 2 * side, side)

    emb_copy = pltpu.make_async_copy(emb_hbm, emb, emb_sem)
    emb_copy.start()

    barrier = pltpu.get_barrier_semaphore()
    for d in range(1, n_row):
        pl.semaphore_signal(
            barrier, inc=1, device_id=(lax.rem(r + d, n_row), p), device_id_type=MESH
        )
    for d in range(1, n_proto):
        pl.semaphore_signal(
            barrier, inc=1, device_id=(r, lax.rem(p + d, n_proto)), device_id_type=MESH
        )
    pl.semaphore_wait(barrier, n_row + n_proto - 2)

    half, quarter = slab // 2, slab // 4
    span = protos // PARTS

    def shift(tree, df, ds):
        return (ds, df) if tree == 0 else (df, ds)

    def piece(n, tree, df, ds, which, ref=None):
        start = tree * half + (quarter if which == "hi" else 0)
        size = half if which == "all" else quarter
        if ref is None:
            ref = feat
            start = pl.multiple_of(row_of(*shift(tree, df, ds)) * slab + start, quarter)
        return ref.at[pl.ds(start, size), n * span : (n + 1) * span]

    slots = {}
    for sign in "+-":
        for key in ("f", "g", "s0", "s-1", "s1", "s2", "t0", "t-1", "t1", "t2"):
            slots[key + sign] = len(slots)
    towards = {"+": 1, "-": -1}

    def gather_copy(n, tree, key, at, which, from_own=False):
        way = towards[key[-1]]
        move = (way, 0) if key[0] in "fg" else (0, way)
        block = piece(n, tree, *at, which)
        return pltpu.make_async_remote_copy(
            src_ref=piece(n, tree, 0, 0, which, own_ref) if from_own else block,
            dst_ref=block,
            send_sem=gs_sem.at[n, tree, slots[key]],
            recv_sem=gr_sem.at[n, tree, slots[key]],
            device_id=(row_of(*shift(tree, *move)), p),
            device_id_type=MESH,
        )

    sent = []

    def push(n, tree, key, at, which, from_own=False):
        copy = gather_copy(n, tree, key, at, which, from_own)
        copy.start()
        sent.append(copy)

    def arrive(n, tree, key, at, which):
        gather_copy(n, tree, key, at, which).wait_recv()

    def across(n, t, df):
        push(n, t, "s%d+" % df, (df, 0), "all")
        push(n, t, "s%d-" % df, (df, 0), "all")

    def relay(n, t, df):
        arrive(n, t, "s%d+" % df, (df, -1), "all")
        push(n, t, "t%d+" % df, (df, -1), "lo")
        arrive(n, t, "s%d-" % df, (df, 1), "all")
        push(n, t, "t%d-" % df, (df, 1), "hi")

    def gather_stage(stage, n):
        if n_row == 1:
            return
        trees = (0, 1)
        if stage == 0:
            for t in trees:
                push(n, t, "f+", (0, 0), "all", True)
                push(n, t, "f-", (0, 0), "all", True)
            for t in trees:
                push(n, t, "s0+", (0, 0), "all", True)
                push(n, t, "s0-", (0, 0), "all", True)
        elif stage == 1:
            for t in trees:
                arrive(n, t, "f+", (-1, 0), "all")
                push(n, t, "g+", (-1, 0), "lo")
                arrive(n, t, "f-", (1, 0), "all")
                push(n, t, "g-", (1, 0), "hi")
            for t in trees:
                across(n, t, -1)
                across(n, t, 1)
        elif stage == 2:
            for t in trees:
                relay(n, t, 0)
        elif stage == 3:
            for t in trees:
                arrive(n, t, "g+", (2, 0), "lo")
                arrive(n, t, "g-", (2, 0), "hi")
                across(n, t, 2)
        elif stage == 4:
            for t in trees:
                relay(n, t, -1)
                relay(n, t, 1)
        elif stage == 5:
            for t in trees:
                relay(n, t, 2)
        elif stage == 6:
            for t in trees:
                for df in (0, -1, 1, 2):
                    arrive(n, t, "t%d+" % df, (df, 2), "lo")
                    arrive(n, t, "t%d-" % df, (df, 2), "hi")

    for n in range(PARTS):
        gather_stage(0, n)
    feat[pl.ds(pl.multiple_of(r * slab, slab), slab), :] = own_ref[...]
    for stage in (1, 2, 3, 4):
        for n in range(PARTS):
            gather_stage(stage, n)
    gather_stage(5, 0)
    gather_stage(6, 0)

    emb_copy.wait()

    mm = min(512, rows // 2)

    def lane_lse(vals):
        peak = tree_reduce(jnp.maximum, vals)
        return peak + jnp.log2(tree_reduce(jnp.add, [jnp.exp2(v - peak) for v in vals]))

    span_tiles = span // TILE

    def score_blocks(n, first, last):
        def block(i, carry):
            row0 = pl.multiple_of(i * mm, mm)
            acc = jnp.dot(
                emb[pl.ds(row0, mm), :],
                feat[:, n * span : (n + 1) * span],
                preferred_element_type=jnp.float32,
            )
            for a in range(mm // TILE):
                bias = [
                    jnp.where(mask_ref[n * span_tiles + j, i * (mm // TILE) + a] == 1, 0.0, NEGATIVE)
                    for j in range(span_tiles)
                ]
                for g in range(a * TILE, (a + 1) * TILE, 8):
                    vals = [
                        acc[g : g + 8, j * TILE : (j + 1) * TILE] * scale + bias[j]
                        for j in range(span_tiles)
                    ]
                    for j in range(span_tiles):
                        col0 = (n * span_tiles + j) * TILE
                        sim[pl.ds(row0 + g, 8), col0 : col0 + TILE] = vals[j]
                    if n > 0:
                        vals.append(wide[pl.ds(row0 + g, 8), :])
                    wide[pl.ds(row0 + g, 8), :] = lane_lse(vals)
            return carry

        lax.fori_loop(first, last, block, 0)

    blocks = rows // mm
    score_blocks(0, 0, max(blocks // 4, 1))
    for n in range(1, PARTS):
        gather_stage(5, n)
    score_blocks(0, max(blocks // 4, 1), blocks)
    for n in range(1, PARTS):
        gather_stage(6, n)

    group = 64

    def lanes(shifts):
        return [jnp.broadcast_to(shifts[j : j + 1, :], (8, TILE)) for j in range(col_tiles)]

    half_rows, half_tiles = rows // 2, row_tiles // 2

    def row_partial(shifts, part):
        def block(step, carry):
            base = pl.multiple_of(step * group, group)
            for g in range(0, group, 8):
                wide[pl.ds(base + g, 8), :] = lane_lse(
                    [sim[pl.ds(base + g, 8), j * TILE : (j + 1) * TILE] + shifts[j] for j in range(col_tiles)]
                )
            return carry

        lax.fori_loop(part * half_rows // group, (part + 1) * half_rows // group, block, 0)

    def row_finish(k, part):
        def block(i, carry):
            t = jnp.transpose(wide[pl.ds(pl.multiple_of(i * TILE, TILE), TILE), :])
            peak = jnp.max(t, axis=0, keepdims=True)
            total = jnp.sum(jnp.exp2(t - peak), axis=0, keepdims=True)
            row_send[k, part, pl.ds(i - part * half_tiles, 1), :] = peak + jnp.log2(total)
            return carry

        lax.fori_loop(part * half_tiles, (part + 1) * half_tiles, block, 0, unroll=4)

    def exchange_start(send, recv, send_sem, recv_sem, at, n, target, near):
        for d in sorted(range(1, n), key=lambda d: (-near(d), d)):
            pltpu.make_async_remote_copy(
                src_ref=send.at[at],
                dst_ref=recv.at[at + (d - 1,)],
                send_sem=send_sem.at[at],
                recv_sem=recv_sem.at[at],
                device_id=target(d),
                device_id_type=MESH,
            ).start()

    def exchange_end(send, recv, send_sem, recv_sem, at, n, target):
        if n > 1:
            pltpu.make_async_remote_copy(
                src_ref=recv.at[at],
                dst_ref=recv.at[at],
                send_sem=send_sem.at[at],
                recv_sem=recv_sem.at[at],
                device_id=target(1),
                device_id_type=MESH,
            ).wait()
        parts = [send[at]] + [recv[at + (d - 1,)] for d in range(1, n)]
        peak = tree_reduce(jnp.maximum, parts)
        total = tree_reduce(jnp.add, [jnp.exp2(v - peak) for v in parts])
        return peak + jnp.log2(total)

    def spread_rows(part):
        def block(i, carry):
            u = jnp.broadcast_to(row_out[pl.ds(i, 1), :], (TILE, TILE))
            wide[pl.ds(pl.multiple_of(i * TILE, TILE), TILE), :] = jnp.transpose(u)
            return carry

        lax.fori_loop(part * half_tiles, (part + 1) * half_tiles, block, 0, unroll=4)

    def column_partial(part, start):
        def block(i, carry):
            base = pl.multiple_of(i * TILE, TILE)
            out = []
            for j in range(col_tiles):
                top, total = carry[j]
                v = sim[pl.ds(base, TILE), j * TILE : (j + 1) * TILE] + wide[pl.ds(base, TILE), :]
                v = v.reshape(TILE // 8, 8, TILE)
                new = jnp.maximum(top, tree_reduce(jnp.maximum, [v[g] for g in range(TILE // 8)]))
                add = tree_reduce(jnp.add, [jnp.exp2(v[g] - new) for g in range(TILE // 8)])
                out.append((new, total * jnp.exp2(top - new) + add))
            return tuple(out)

        return lax.fori_loop(part * half_tiles, (part + 1) * half_tiles, block, start)

    def column_finish(k, done):
        for j in range(col_tiles):
            level = done[j][0] + jnp.log2(done[j][1])
            peak = jnp.max(level, axis=0, keepdims=True)
            total = jnp.sum(jnp.exp2(level - peak), axis=0, keepdims=True)
            col_send[k, j : j + 1, :] = peak + jnp.log2(total)

    def proto_peer(d):
        return (r, lax.rem(p + d, n_proto))

    def row_peer(d):
        return (lax.rem(r + d, n_row), p)

    def wrap(d, n):
        return min(d, n - d)

    row_refs = (row_send, row_recv, rs_sem, rr_sem)
    col_refs = (col_send, col_recv, cs_sem, cr_sem)

    def row_near(d):
        return wrap(d, n_proto)

    def col_near(d):
        return wrap(d // side, side) + wrap(d % side, side)

    shifts = None
    for k in range(ITERS):
        for i in range(2):
            if k > 0:
                row_partial(shifts, i)
            else:
                for n in range(1, PARTS):
                    score_blocks(n, i * half_rows // mm, (i + 1) * half_rows // mm)
            row_finish(k, i)
            exchange_start(*row_refs, (k, i), n_proto, proto_peer, row_near)
        if k == 0:
            for i in range(0, protos, TILE):
                for j in range(0, depth, TILE):
                    feat_t[i : i + TILE, j : j + TILE] = jnp.transpose(feat[j : j + TILE, i : i + TILE])
        columns = tuple(
            (jnp.full((8, TILE), LOWEST, jnp.float32), jnp.zeros((8, TILE), jnp.float32))
            for _ in range(col_tiles)
        )
        for i in range(2):
            row_out[i * half_tiles : (i + 1) * half_tiles, :] = -exchange_end(
                *row_refs, (k, i), n_proto, proto_peer
            )
            spread_rows(i)
            columns = column_partial(i, columns)
        column_finish(k, columns)
        exchange_start(*col_refs, (k,), n_row, row_peer, col_near)
        potential = log_column - exchange_end(*col_refs, (k,), n_row, row_peer)
        shifts = lanes(potential)

    col_out[...] = potential * LN2

    plan = emb
    far = n_z // 2
    order = [far] + [t for d in range(far - 1, 0, -1) for t in (d, n_z - d)] + [0] if far else [0]
    pairs = [order[i : i + 2] for i in range(0, len(order), 2)]
    width = rows // SPLIT
    mp = rows // 2
    sent_sibling = []

    def plan_block(base):
        for g in range(0, mp, 16):
            shift = [wide[pl.ds(base + g + e, 8), :] for e in (0, 8)]
            for j in range(col_tiles):
                v = [
                    jnp.exp2(sim[pl.ds(base + g + e, 8), j * TILE : (j + 1) * TILE] + (shift[e // 8] + shifts[j]))
                    for e in (0, 8)
                ]
                plan[pl.ds(base + g, 16), j * TILE : (j + 1) * TILE] = jnp.concatenate(v, axis=0).astype(
                    jnp.bfloat16
                )

    def product(ts, base):
        weights = [
            feat_t[:, pl.ds(pl.multiple_of(lax.rem(z + t, n_z) * 2 * share, 2 * share), 2 * share)] for t in ts
        ]
        acc = jnp.dot(
            plan[pl.ds(base, mp), :],
            jnp.concatenate(weights, axis=1) if len(ts) > 1 else weights[0],
            preferred_element_type=jnp.float32,
        )
        for i, t in enumerate(ts):
            part[t, :, pl.ds(base, mp)] = jnp.transpose(acc[:, i * 2 * share : (i + 1) * 2 * share]).astype(
                jnp.bfloat16
            )

    def sibling_copy(t, h):
        other = 1 - c
        return pltpu.make_async_remote_copy(
            src_ref=part.at[t, pl.ds(pl.multiple_of(other * share, share), share), h * width : (h + 1) * width],
            dst_ref=sib_recv.at[t, h],
            send_sem=ss_sem.at[t, h],
            recv_sem=sr_sem.at[t, h],
            device_id=(r, z * 2 + other),
            device_id_type=MESH,
        )

    def to_sibling(ts, hs):
        for t in ts:
            for h in hs:
                copy = sibling_copy(t, h)
                copy.start()
                sent_sibling.append(copy)

    def chip_sum(t, h):
        sibling_copy(t, h).wait_recv()
        mine = part[t, pl.ds(pl.multiple_of(c * share, share), share), h * width : (h + 1) * width]
        return mine.astype(jnp.float32) + sib_recv[t, h].astype(jnp.float32)

    def chain_copy(way, d, h):
        step = 1 if way == 0 else n_z - 1
        return pltpu.make_async_remote_copy(
            src_ref=tx.at[way, d - 1, h],
            dst_ref=rx.at[way, d - 1, h],
            send_sem=ts_sem.at[way, d - 1, h],
            recv_sem=tr_sem.at[way, d - 1, h],
            device_id=(r, lax.rem(z + step, n_z) * 2 + c),
            device_id_type=MESH,
        )

    flying = []
    lower, upper = list(range(SPLIT // 2)), list(range(SPLIT // 2, SPLIT))
    whole_way = (lower, upper)
    rest = (upper, lower)

    def forward(way, d, hs):
        t = d if way == 0 else n_z - d
        for h in hs:
            value = chip_sum(t, h)
            if d < far and (d + 1 < far or h in whole_way[way]):
                chain_copy(way, d + 1, h).wait_recv()
                value = value + rx[way, d, h].astype(jnp.float32)
            tx[way, d - 1, h] = value.astype(jnp.bfloat16)
            copy = chain_copy(way, d, h)
            copy.start()
            flying.append(copy)

    def later_pair(n):
        if n < len(pairs):

            def block(i, carry):
                product(pairs[n], pl.multiple_of(i * mp, mp))
                return carry

            lax.fori_loop(0, 2, block, 0)
            to_sibling(pairs[n], lower + upper)

    for i, hs in enumerate((lower, upper)):
        plan_block(i * mp)
        product(pairs[0], i * mp)
        to_sibling(pairs[0], hs)
    if far:
        forward(0, far, lower)
        forward(1, far, upper)
    if far > 1:
        forward(0, far - 1, upper)
    later_pair(1)
    if far > 1:
        forward(1, far - 1, lower)
    later_pair(2)
    if far > 1:
        forward(0, far - 1, lower)
        forward(1, far - 1, upper)
    later_pair(3)
    for d in range(far - 2, 0, -1):
        for h, g in zip(upper + lower, lower + upper):
            forward(0, d, [h])
            forward(1, d, [g])
    for h in upper + lower:
        value = chip_sum(0, h)
        for way in (0, 1):
            if far > 1 or (far == 1 and h in whole_way[way]):
                chain_copy(way, 1, h).wait_recv()
                value = value + rx[way, 0, h].astype(jnp.float32)
        out_ref[:, h * width : (h + 1) * width] = value.astype(jnp.bfloat16)
    row_out[...] = row_out[...] * LN2

    for copy in sent + sent_sibling + flying:
        copy.wait_send()


def hand_over(a, b, c, a_out, b_out, c_out):
    a_out[...] = a[...]
    b_out[...] = b[...]
    c_out[...] = c[...]


def solution(mesh):
    n_row, n_proto = mesh.shape["row"], mesh.shape["proto"]
    side = math.isqrt(n_row)
    n_z = n_proto // 2
    far = max(n_z // 2, 1)

    def shards(embeddings, prototypes, block_mask):
        rows, depth = embeddings.shape
        protos, slab = prototypes.shape
        share = depth // n_proto
        row_tiles, col_tiles = rows // TILE, protos // TILE
        log_column = math.log2((rows * n_row) / (protos * n_proto))
        f32, bf16 = jnp.float32, jnp.bfloat16
        dma = pltpu.SemaphoreType.DMA
        peers_r, peers_p = max(n_row - 1, 1), max(n_proto - 1, 1)
        vmem = pl.BlockSpec(memory_space=pltpu.VMEM)
        shapes = (
            jax.ShapeDtypeStruct((share, rows), bf16),
            jax.ShapeDtypeStruct((row_tiles, TILE), f32),
            jax.ShapeDtypeStruct((col_tiles, TILE), f32),
        )
        results = pl.pallas_call(
            functools.partial(kernel, (side, n_row, n_proto, log_column)),
            out_shape=shapes,
            in_specs=[
                vmem,
                pl.BlockSpec(memory_space=pl.ANY),
                pl.BlockSpec(memory_space=pltpu.SMEM),
            ],
            out_specs=(vmem, vmem, vmem),
            scratch_shapes=[
                pltpu.VMEM((rows, depth), bf16),
                pltpu.VMEM((depth, protos), bf16),
                pltpu.VMEM((protos, depth), bf16),
                pltpu.VMEM((rows, protos), f32),
                pltpu.VMEM((rows, TILE), f32),
                pltpu.VMEM((ITERS, 2, row_tiles // 2, TILE), f32),
                pltpu.VMEM((ITERS, 2, peers_p, row_tiles // 2, TILE), f32),
                pltpu.VMEM((ITERS, col_tiles, TILE), f32),
                pltpu.VMEM((ITERS, peers_r, col_tiles, TILE), f32),
                pltpu.VMEM((n_z, 2 * share, rows), bf16),
                pltpu.VMEM((n_z, SPLIT, share, rows // SPLIT), bf16),
                pltpu.VMEM((2, far, SPLIT, share, rows // SPLIT), bf16),
                pltpu.VMEM((2, far, SPLIT, share, rows // SPLIT), bf16),
                dma(()),
                dma((PARTS, 2, 20)),
                dma((PARTS, 2, 20)),
                dma((ITERS, 2)),
                dma((ITERS, 2)),
                dma((ITERS,)),
                dma((ITERS,)),
                dma((n_z, SPLIT)),
                dma((n_z, SPLIT)),
                dma((2, far, SPLIT)),
                dma((2, far, SPLIT)),
            ],
            compiler_params=pltpu.CompilerParams(
                collective_id=0, has_side_effects=True, vmem_limit_bytes=56 * 1024 * 1024
            ),
        )(prototypes.T, embeddings, block_mask.T)
        targets, row_potential, column_potential = pl.pallas_call(hand_over, out_shape=shapes)(*results)
        return (
            targets.T,
            row_potential.reshape(rows),
            column_potential.reshape(protos),
        )

    return jax.shard_map(
        shards,
        mesh=mesh,
        in_specs=(P("row", None), P("proto", "row"), P("row", "proto")),
        out_specs=(P("row", "proto"), P("row"), P("proto")),
        check_vma=False,
    )
```

```python
import functools
import math

import jax
import jax.numpy as jnp
from jax import lax
from jax.experimental import pallas as pl
from jax.experimental.pallas import tpu as pltpu
from jax.sharding import PartitionSpec as P

ITERS = 3
TILE = 128
NEGATIVE = -1e30
LOWEST = -1e38
LOG2E = 1.4426950408889634
LN2 = 0.6931471805599453
SPLIT = 4
PARTS = 1
MESH = pl.DeviceIdType.MESH


def tree_reduce(op, parts):
    while len(parts) > 1:
        pairs = [op(parts[i], parts[i + 1]) for i in range(0, len(parts) - 1, 2)]
        parts = pairs + ([parts[-1]] if len(parts) % 2 else [])
    return parts[0]


def kernel(
    cfg,
    own_ref,
    emb_hbm,
    mask_ref,
    out_ref,
    row_out,
    col_out,
    emb,
    feat,
    feat_t,
    sim,
    wide,
    row_send,
    row_recv,
    col_send,
    col_recv,
    part,
    sib_recv,
    tx,
    rx,
    emb_sem,
    gs_sem,
    gr_sem,
    rs_sem,
    rr_sem,
    cs_sem,
    cr_sem,
    ss_sem,
    sr_sem,
    ts_sem,
    tr_sem,
    hello_sem,
):
    side, n_row, n_proto, log_column = cfg
    n_z = n_proto // 2
    slab, protos = own_ref.shape
    share = out_ref.shape[0]
    depth = feat.shape[0]
    rows = sim.shape[0]
    row_tiles, col_tiles = rows // TILE, protos // TILE
    scale = 4.0 / math.sqrt(depth) * LOG2E

    r = lax.axis_index("row")
    p = lax.axis_index("proto")
    y, x = r // side, lax.rem(r, side)
    z, c = p // 2, lax.rem(p, 2)

    def row_of(dy, dx):
        return lax.rem(y + dy + 2 * side, side) * side + lax.rem(x + dx + 2 * side, side)

    emb_copy = pltpu.make_async_copy(emb_hbm, emb, emb_sem)
    emb_copy.start()

    neighbours = [(r, z * 2 + 1 - c)]
    if n_row > 1:
        for move in ((0, 1), (0, -1), (1, 0), (-1, 0)):
            neighbours.append((row_of(*move), p))
    up, down = lax.rem(z + 1, n_z), lax.rem(z + n_z - 1, n_z)
    if n_z > 1:
        for side_z in (up, down):
            neighbours.extend([(r, side_z * 2 + c), (r, side_z * 2 + 1 - c)])
    barrier = pltpu.get_barrier_semaphore()
    for peer in neighbours:
        pl.semaphore_signal(barrier, inc=1, device_id=peer, device_id_type=MESH)
    pl.semaphore_wait(barrier, len(neighbours))

    def hello(i):
        if n_z // 2 > i + 1:
            for side_z in (up, down):
                pl.semaphore_signal(
                    hello_sem.at[i], inc=1, device_id=(r, side_z * 2 + c), device_id_type=MESH
                )

    def hello_end(i):
        if n_z // 2 > i + 1:
            pl.semaphore_wait(hello_sem.at[i], 2)

    half, quarter = slab // 2, slab // 4
    span = protos // PARTS

    def shift(tree, df, ds):
        return (ds, df) if tree == 0 else (df, ds)

    def piece(n, tree, df, ds, which, ref=None):
        start = tree * half + (quarter if which == "hi" else 0)
        size = half if which == "all" else quarter
        if ref is None:
            ref = feat
            start = pl.multiple_of(row_of(*shift(tree, df, ds)) * slab + start, quarter)
        return ref.at[pl.ds(start, size), n * span : (n + 1) * span]

    slots = {}
    for sign in "+-":
        for key in ("f", "g", "s0", "s-1", "s1", "s2", "t0", "t-1", "t1", "t2"):
            slots[key + sign] = len(slots)
    towards = {"+": 1, "-": -1}

    def gather_copy(n, tree, key, at, which, from_own=False):
        way = towards[key[-1]]
        move = (way, 0) if key[0] in "fg" else (0, way)
        block = piece(n, tree, *at, which)
        return pltpu.make_async_remote_copy(
            src_ref=piece(n, tree, 0, 0, which, own_ref) if from_own else block,
            dst_ref=block,
            send_sem=gs_sem.at[n, tree, slots[key]],
            recv_sem=gr_sem.at[n, tree, slots[key]],
            device_id=(row_of(*shift(tree, *move)), p),
            device_id_type=MESH,
        )

    sent = []

    def push(n, tree, key, at, which, from_own=False):
        copy = gather_copy(n, tree, key, at, which, from_own)
        copy.start()
        sent.append(copy)

    def arrive(n, tree, key, at, which):
        gather_copy(n, tree, key, at, which).wait_recv()

    def across(n, t, df):
        push(n, t, "s%d+" % df, (df, 0), "all")
        push(n, t, "s%d-" % df, (df, 0), "all")

    def relay(n, t, df):
        arrive(n, t, "s%d+" % df, (df, -1), "all")
        push(n, t, "t%d+" % df, (df, -1), "lo")
        arrive(n, t, "s%d-" % df, (df, 1), "all")
        push(n, t, "t%d-" % df, (df, 1), "hi")

    def gather_stage(stage, n):
        if n_row == 1:
            return
        trees = (0, 1)
        if stage == 0:
            for t in trees:
                push(n, t, "f+", (0, 0), "all", True)
                push(n, t, "f-", (0, 0), "all", True)
            for t in trees:
                push(n, t, "s0+", (0, 0), "all", True)
                push(n, t, "s0-", (0, 0), "all", True)
        elif stage == 1:
            for t in trees:
                arrive(n, t, "f+", (-1, 0), "all")
                push(n, t, "g+", (-1, 0), "lo")
                arrive(n, t, "f-", (1, 0), "all")
                push(n, t, "g-", (1, 0), "hi")
            for t in trees:
                across(n, t, -1)
                across(n, t, 1)
        elif stage == 2:
            for t in trees:
                relay(n, t, 0)
        elif stage == 3:
            for t in trees:
                arrive(n, t, "g+", (2, 0), "lo")
                arrive(n, t, "g-", (2, 0), "hi")
                across(n, t, 2)
        elif stage == 4:
            for t in trees:
                relay(n, t, -1)
                relay(n, t, 1)
        elif stage == 5:
            for t in trees:
                relay(n, t, 2)
        elif stage == 6:
            for t in trees:
                for df in (0, -1, 1, 2):
                    arrive(n, t, "t%d+" % df, (df, 2), "lo")
                    arrive(n, t, "t%d-" % df, (df, 2), "hi")

    for n in range(PARTS):
        gather_stage(0, n)
    hello(0)
    feat[pl.ds(pl.multiple_of(r * slab, slab), slab), :] = own_ref[...]
    for stage in (1, 2, 3, 4):
        for n in range(PARTS):
            gather_stage(stage, n)
        if stage < 4:
            hello_end(stage - 1)
            if stage < 3:
                hello(stage)
    gather_stage(5, 0)
    gather_stage(6, 0)

    emb_copy.wait()

    mm = min(512, rows // 2)

    def lane_lse(vals):
        peak = tree_reduce(jnp.maximum, vals)
        return peak + jnp.log2(tree_reduce(jnp.add, [jnp.exp2(v - peak) for v in vals]))

    span_tiles = span // TILE

    def score_blocks(n, first, last):
        def block(i, carry):
            row0 = pl.multiple_of(i * mm, mm)
            acc = jnp.dot(
                emb[pl.ds(row0, mm), :],
                feat[:, n * span : (n + 1) * span],
                preferred_element_type=jnp.float32,
            )
            for a in range(mm // TILE):
                bias = [
                    jnp.where(mask_ref[n * span_tiles + j, i * (mm // TILE) + a] == 1, 0.0, NEGATIVE)
                    for j in range(span_tiles)
                ]
                for g in range(a * TILE, (a + 1) * TILE, 8):
                    vals = [
                        acc[g : g + 8, j * TILE : (j + 1) * TILE] * scale + bias[j]
                        for j in range(span_tiles)
                    ]
                    for j in range(span_tiles):
                        col0 = (n * span_tiles + j) * TILE
                        sim[pl.ds(row0 + g, 8), col0 : col0 + TILE] = vals[j]
                    if n > 0:
                        vals.append(wide[pl.ds(row0 + g, 8), :])
                    wide[pl.ds(row0 + g, 8), :] = lane_lse(vals)
            return carry

        lax.fori_loop(first, last, block, 0)

    blocks = rows // mm
    if PARTS > 1:
        score_blocks(0, 0, max(blocks // 4, 1))
        for n in range(1, PARTS):
            gather_stage(5, n)
        score_blocks(0, max(blocks // 4, 1), blocks)
        for n in range(1, PARTS):
            gather_stage(6, n)

    group = 64

    def lanes(shifts):
        return [jnp.broadcast_to(shifts[j : j + 1, :], (8, TILE)) for j in range(col_tiles)]

    half_rows, half_tiles = rows // 2, row_tiles // 2

    def row_partial(shifts, part):
        def block(step, carry):
            base = pl.multiple_of(step * group, group)
            for g in range(0, group, 8):
                wide[pl.ds(base + g, 8), :] = lane_lse(
                    [sim[pl.ds(base + g, 8), j * TILE : (j + 1) * TILE] + shifts[j] for j in range(col_tiles)]
                )
            return carry

        lax.fori_loop(part * half_rows // group, (part + 1) * half_rows // group, block, 0)

    def row_finish(k, part):
        def block(i, carry):
            t = jnp.transpose(wide[pl.ds(pl.multiple_of(i * TILE, TILE), TILE), :])
            peak = jnp.max(t, axis=0, keepdims=True)
            total = jnp.sum(jnp.exp2(t - peak), axis=0, keepdims=True)
            row_send[k, part, pl.ds(i - part * half_tiles, 1), :] = peak + jnp.log2(total)
            return carry

        lax.fori_loop(part * half_tiles, (part + 1) * half_tiles, block, 0, unroll=4)

    def exchange_start(send, recv, send_sem, recv_sem, at, n, target, near):
        for d in sorted(range(1, n), key=lambda d: (-near(d), d)):
            pltpu.make_async_remote_copy(
                src_ref=send.at[at],
                dst_ref=recv.at[at + (d - 1,)],
                send_sem=send_sem.at[at],
                recv_sem=recv_sem.at[at],
                device_id=target(d),
                device_id_type=MESH,
            ).start()

    def exchange_end(send, recv, send_sem, recv_sem, at, n, target):
        if n > 1:
            pltpu.make_async_remote_copy(
                src_ref=recv.at[at],
                dst_ref=recv.at[at],
                send_sem=send_sem.at[at],
                recv_sem=recv_sem.at[at],
                device_id=target(1),
                device_id_type=MESH,
            ).wait()
        parts = [send[at]] + [recv[at + (d - 1,)] for d in range(1, n)]
        peak = tree_reduce(jnp.maximum, parts)
        total = tree_reduce(jnp.add, [jnp.exp2(v - peak) for v in parts])
        return peak + jnp.log2(total)

    def spread_rows(part):
        def block(i, carry):
            u = jnp.broadcast_to(row_out[pl.ds(i, 1), :], (TILE, TILE))
            wide[pl.ds(pl.multiple_of(i * TILE, TILE), TILE), :] = jnp.transpose(u)
            return carry

        lax.fori_loop(part * half_tiles, (part + 1) * half_tiles, block, 0, unroll=4)

    def column_partial(part, start):
        def block(i, carry):
            base = pl.multiple_of(i * TILE, TILE)
            out = []
            for j in range(col_tiles):
                top, total = carry[j]
                v = sim[pl.ds(base, TILE), j * TILE : (j + 1) * TILE] + wide[pl.ds(base, TILE), :]
                v = v.reshape(TILE // 8, 8, TILE)
                new = jnp.maximum(top, tree_reduce(jnp.maximum, [v[g] for g in range(TILE // 8)]))
                add = tree_reduce(jnp.add, [jnp.exp2(v[g] - new) for g in range(TILE // 8)])
                out.append((new, total * jnp.exp2(top - new) + add))
            return tuple(out)

        return lax.fori_loop(part * half_tiles, (part + 1) * half_tiles, block, start)

    def column_finish(k, done):
        for j in range(col_tiles):
            level = done[j][0] + jnp.log2(done[j][1])
            peak = jnp.max(level, axis=0, keepdims=True)
            total = jnp.sum(jnp.exp2(level - peak), axis=0, keepdims=True)
            col_send[k, j : j + 1, :] = peak + jnp.log2(total)

    def proto_peer(d):
        return (r, lax.rem(p + d, n_proto))

    def row_peer(d):
        return (lax.rem(r + d, n_row), p)

    def wrap(d, n):
        return min(d, n - d)

    row_refs = (row_send, row_recv, rs_sem, rr_sem)
    col_refs = (col_send, col_recv, cs_sem, cr_sem)

    def row_near(d):
        return wrap(d, n_proto)

    def col_near(d):
        return wrap(d // side, side) + wrap(d % side, side)

    shifts = None
    for k in range(ITERS):
        for i in range(2):
            if k > 0:
                row_partial(shifts, i)
            else:
                for n in range(min(1, PARTS - 1), PARTS):
                    score_blocks(n, i * half_rows // mm, (i + 1) * half_rows // mm)
            row_finish(k, i)
            exchange_start(*row_refs, (k, i), n_proto, proto_peer, row_near)
        if k == 0:
            for i in range(0, protos, TILE):
                for j in range(0, depth, TILE):
                    feat_t[i : i + TILE, j : j + TILE] = jnp.transpose(feat[j : j + TILE, i : i + TILE])
        columns = tuple(
            (jnp.full((8, TILE), LOWEST, jnp.float32), jnp.zeros((8, TILE), jnp.float32))
            for _ in range(col_tiles)
        )
        for i in range(2):
            row_out[i * half_tiles : (i + 1) * half_tiles, :] = -exchange_end(
                *row_refs, (k, i), n_proto, proto_peer
            )
            spread_rows(i)
            columns = column_partial(i, columns)
        column_finish(k, columns)
        exchange_start(*col_refs, (k,), n_row, row_peer, col_near)
        potential = log_column - exchange_end(*col_refs, (k,), n_row, row_peer)
        shifts = lanes(potential)

    col_out[...] = potential * LN2

    plan = emb
    far = n_z // 2
    order = [far] + [t for d in range(far - 1, 0, -1) for t in (d, n_z - d)] + [0] if far else [0]
    pairs = [order[i : i + 2] for i in range(0, len(order), 2)]
    width = rows // SPLIT
    mp = rows // 2
    sent_sibling = []

    def plan_block(base):
        for g in range(0, mp, 16):
            shift = [wide[pl.ds(base + g + e, 8), :] for e in (0, 8)]
            for j in range(col_tiles):
                v = [
                    jnp.exp2(sim[pl.ds(base + g + e, 8), j * TILE : (j + 1) * TILE] + (shift[e // 8] + shifts[j]))
                    for e in (0, 8)
                ]
                plan[pl.ds(base + g, 16), j * TILE : (j + 1) * TILE] = jnp.concatenate(v, axis=0).astype(
                    jnp.bfloat16
                )

    def product(ts, base):
        weights = [
            feat_t[:, pl.ds(pl.multiple_of(lax.rem(z + t, n_z) * 2 * share, 2 * share), 2 * share)] for t in ts
        ]
        acc = jnp.dot(
            plan[pl.ds(base, mp), :],
            jnp.concatenate(weights, axis=1) if len(ts) > 1 else weights[0],
            preferred_element_type=jnp.float32,
        )
        for i, t in enumerate(ts):
            part[t, :, pl.ds(base, mp)] = jnp.transpose(acc[:, i * 2 * share : (i + 1) * 2 * share]).astype(
                jnp.bfloat16
            )

    def sibling_copy(t, h):
        other = 1 - c
        return pltpu.make_async_remote_copy(
            src_ref=part.at[t, pl.ds(pl.multiple_of(other * share, share), share), h * width : (h + 1) * width],
            dst_ref=sib_recv.at[t, h],
            send_sem=ss_sem.at[t, h],
            recv_sem=sr_sem.at[t, h],
            device_id=(r, z * 2 + other),
            device_id_type=MESH,
        )

    def to_sibling(ts, hs):
        for t in ts:
            for h in hs:
                copy = sibling_copy(t, h)
                copy.start()
                sent_sibling.append(copy)

    def chip_sum(t, h):
        sibling_copy(t, h).wait_recv()
        mine = part[t, pl.ds(pl.multiple_of(c * share, share), share), h * width : (h + 1) * width]
        return mine.astype(jnp.float32) + sib_recv[t, h].astype(jnp.float32)

    def chain_copy(way, d, h):
        step = 1 if way == 0 else n_z - 1
        return pltpu.make_async_remote_copy(
            src_ref=tx.at[way, d - 1, h],
            dst_ref=rx.at[way, d - 1, h],
            send_sem=ts_sem.at[way, d - 1, h],
            recv_sem=tr_sem.at[way, d - 1, h],
            device_id=(r, lax.rem(z + step, n_z) * 2 + c),
            device_id_type=MESH,
        )

    flying = []
    lower, upper = list(range(SPLIT // 2)), list(range(SPLIT // 2, SPLIT))
    whole_way = (lower, upper)
    rest = (upper, lower)

    def forward(way, d, hs):
        t = d if way == 0 else n_z - d
        for h in hs:
            value = chip_sum(t, h)
            if d < far and (d + 1 < far or h in whole_way[way]):
                chain_copy(way, d + 1, h).wait_recv()
                value = value + rx[way, d, h].astype(jnp.float32)
            tx[way, d - 1, h] = value.astype(jnp.bfloat16)
            copy = chain_copy(way, d, h)
            copy.start()
            flying.append(copy)

    def later_pair(n):
        if n < len(pairs):

            def block(i, carry):
                product(pairs[n], pl.multiple_of(i * mp, mp))
                return carry

            lax.fori_loop(0, 2, block, 0)
            to_sibling(pairs[n], lower + upper)

    for i, hs in enumerate((lower, upper)):
        plan_block(i * mp)
        product(pairs[0], i * mp)
        to_sibling(pairs[0], hs)
    if far:
        forward(0, far, lower)
        forward(1, far, upper)
    if far > 1:
        forward(0, far - 1, upper)
    later_pair(1)
    if far > 1:
        forward(1, far - 1, lower)
    later_pair(2)
    if far > 1:
        forward(0, far - 1, lower)
        forward(1, far - 1, upper)
    later_pair(3)
    for d in range(far - 2, 0, -1):
        for h, g in zip(upper + lower, lower + upper):
            forward(0, d, [h])
            forward(1, d, [g])
    for h in upper + lower:
        value = chip_sum(0, h)
        for way in (0, 1):
            if far > 1 or (far == 1 and h in whole_way[way]):
                chain_copy(way, 1, h).wait_recv()
                value = value + rx[way, 0, h].astype(jnp.float32)
        out_ref[:, h * width : (h + 1) * width] = value.astype(jnp.bfloat16)
    row_out[...] = row_out[...] * LN2

    for copy in sent + sent_sibling + flying:
        copy.wait_send()


def hand_over(a, b, c, a_out, b_out, c_out):
    a_out[...] = a[...]
    b_out[...] = b[...]
    c_out[...] = c[...]


def solution(mesh):
    n_row, n_proto = mesh.shape["row"], mesh.shape["proto"]
    side = math.isqrt(n_row)
    n_z = n_proto // 2
    far = max(n_z // 2, 1)

    def shards(embeddings, prototypes, block_mask):
        rows, depth = embeddings.shape
        protos, slab = prototypes.shape
        share = depth // n_proto
        row_tiles, col_tiles = rows // TILE, protos // TILE
        log_column = math.log2((rows * n_row) / (protos * n_proto))
        f32, bf16 = jnp.float32, jnp.bfloat16
        dma = pltpu.SemaphoreType.DMA
        peers_r, peers_p = max(n_row - 1, 1), max(n_proto - 1, 1)
        vmem = pl.BlockSpec(memory_space=pltpu.VMEM)
        shapes = (
            jax.ShapeDtypeStruct((share, rows), bf16),
            jax.ShapeDtypeStruct((row_tiles, TILE), f32),
            jax.ShapeDtypeStruct((col_tiles, TILE), f32),
        )
        results = pl.pallas_call(
            functools.partial(kernel, (side, n_row, n_proto, log_column)),
            out_shape=shapes,
            in_specs=[
                vmem,
                pl.BlockSpec(memory_space=pl.ANY),
                pl.BlockSpec(memory_space=pltpu.SMEM),
            ],
            out_specs=(vmem, vmem, vmem),
            scratch_shapes=[
                pltpu.VMEM((rows, depth), bf16),
                pltpu.VMEM((depth, protos), bf16),
                pltpu.VMEM((protos, depth), bf16),
                pltpu.VMEM((rows, protos), f32),
                pltpu.VMEM((rows, TILE), f32),
                pltpu.VMEM((ITERS, 2, row_tiles // 2, TILE), f32),
                pltpu.VMEM((ITERS, 2, peers_p, row_tiles // 2, TILE), f32),
                pltpu.VMEM((ITERS, col_tiles, TILE), f32),
                pltpu.VMEM((ITERS, peers_r, col_tiles, TILE), f32),
                pltpu.VMEM((n_z, 2 * share, rows), bf16),
                pltpu.VMEM((n_z, SPLIT, share, rows // SPLIT), bf16),
                pltpu.VMEM((2, far, SPLIT, share, rows // SPLIT), bf16),
                pltpu.VMEM((2, far, SPLIT, share, rows // SPLIT), bf16),
                dma(()),
                dma((PARTS, 2, 20)),
                dma((PARTS, 2, 20)),
                dma((ITERS, 2)),
                dma((ITERS, 2)),
                dma((ITERS,)),
                dma((ITERS,)),
                dma((n_z, SPLIT)),
                dma((n_z, SPLIT)),
                dma((2, far, SPLIT)),
                dma((2, far, SPLIT)),
                pltpu.SemaphoreType.REGULAR((3,)),
            ],
            compiler_params=pltpu.CompilerParams(
                collective_id=0, has_side_effects=True, vmem_limit_bytes=56 * 1024 * 1024
            ),
        )(prototypes.T, embeddings, block_mask.T)
        targets, row_potential, column_potential = pl.pallas_call(hand_over, out_shape=shapes)(*results)
        return (
            targets.T,
            row_potential.reshape(rows),
            column_potential.reshape(protos),
        )

    return jax.shard_map(
        shards,
        mesh=mesh,
        in_specs=(P("row", None), P("proto", "row"), P("row", "proto")),
        out_specs=(P("row", "proto"), P("row"), P("proto")),
        check_vma=False,
    )
```

```python
import functools
import math

import jax
import jax.numpy as jnp
from jax import lax
from jax.experimental import pallas as pl
from jax.experimental.pallas import tpu as pltpu
from jax.sharding import PartitionSpec as P

ITERS = 3
TILE = 128
NEGATIVE = -1e30
LOWEST = -1e38
LOG2E = 1.4426950408889634
LN2 = 0.6931471805599453
SPLIT = 2
PARTS = 1
MESH = pl.DeviceIdType.MESH


def tree_reduce(op, parts):
    while len(parts) > 1:
        pairs = [op(parts[i], parts[i + 1]) for i in range(0, len(parts) - 1, 2)]
        parts = pairs + ([parts[-1]] if len(parts) % 2 else [])
    return parts[0]


def kernel(
    cfg,
    own_ref,
    emb_hbm,
    mask_ref,
    out_ref,
    row_out,
    col_out,
    emb,
    feat,
    feat_t,
    sim,
    wide,
    row_send,
    row_recv,
    col_send,
    col_recv,
    part,
    sib_recv,
    tx,
    rx,
    emb_sem,
    own_sem,
    gs_sem,
    gr_sem,
    rs_sem,
    rr_sem,
    cs_sem,
    cr_sem,
    ss_sem,
    sr_sem,
    ts_sem,
    tr_sem,
    hello_sem,
):
    side, n_row, n_proto, log_column = cfg
    n_z = n_proto // 2
    slab, protos = own_ref.shape
    share = out_ref.shape[0]
    depth = feat.shape[0]
    rows = sim.shape[0]
    row_tiles, col_tiles = rows // TILE, protos // TILE
    scale = 4.0 / math.sqrt(depth) * LOG2E

    r = lax.axis_index("row")
    p = lax.axis_index("proto")
    y, x = r // side, lax.rem(r, side)
    z, c = p // 2, lax.rem(p, 2)

    def row_of(dy, dx):
        return lax.rem(y + dy + 2 * side, side) * side + lax.rem(x + dx + 2 * side, side)


    neighbours = [(r, z * 2 + 1 - c)]
    if n_row > 1:
        for move in ((0, 1), (0, -1), (1, 0), (-1, 0)):
            neighbours.append((row_of(*move), p))
    up, down = lax.rem(z + 1, n_z), lax.rem(z + n_z - 1, n_z)
    if n_z > 1:
        for side_z in (up, down):
            neighbours.extend([(r, side_z * 2 + c), (r, side_z * 2 + 1 - c)])
    barrier = pltpu.get_barrier_semaphore()
    for peer in neighbours:
        pl.semaphore_signal(barrier, inc=1, device_id=peer, device_id_type=MESH)
    pl.semaphore_wait(barrier, len(neighbours))

    def hello(i):
        if n_z // 2 > i + 1:
            for side_z in (up, down):
                pl.semaphore_signal(
                    hello_sem.at[i], inc=1, device_id=(r, side_z * 2 + c), device_id_type=MESH
                )

    def hello_end(i):
        if n_z // 2 > i + 1:
            pl.semaphore_wait(hello_sem.at[i], 2)

    own_rows = pl.ds(pl.multiple_of(r * slab, slab), slab)
    own_copy = pltpu.make_async_copy(own_ref, feat.at[own_rows, :], own_sem)
    own_copy.start()

    half, quarter = slab // 2, slab // 4
    span = protos // PARTS

    def shift(tree, df, ds):
        return (ds, df) if tree == 0 else (df, ds)

    def piece(n, tree, df, ds, which, ref=None):
        start = tree * half + (quarter if which == "hi" else 0)
        size = half if which == "all" else quarter
        if ref is None:
            ref = feat
            start = pl.multiple_of(row_of(*shift(tree, df, ds)) * slab + start, quarter)
        return ref.at[pl.ds(start, size), n * span : (n + 1) * span]

    slots = {}
    for sign in "+-":
        for key in ("f", "g", "s0", "s-1", "s1", "s2", "t0", "t-1", "t1", "t2"):
            slots[key + sign] = len(slots)
    towards = {"+": 1, "-": -1}

    def gather_copy(n, tree, key, at, which, from_own=False):
        way = towards[key[-1]]
        move = (way, 0) if key[0] in "fg" else (0, way)
        block = piece(n, tree, *at, which)
        return pltpu.make_async_remote_copy(
            src_ref=piece(n, tree, 0, 0, which, own_ref) if from_own else block,
            dst_ref=block,
            send_sem=gs_sem.at[n, tree, slots[key]],
            recv_sem=gr_sem.at[n, tree, slots[key]],
            device_id=(row_of(*shift(tree, *move)), p),
            device_id_type=MESH,
        )

    sent = []

    def push(n, tree, key, at, which, from_own=False):
        copy = gather_copy(n, tree, key, at, which, from_own)
        copy.start()
        sent.append(copy)

    def arrive(n, tree, key, at, which):
        gather_copy(n, tree, key, at, which).wait_recv()

    def across(n, t, df):
        push(n, t, "s%d+" % df, (df, 0), "all")
        push(n, t, "s%d-" % df, (df, 0), "all")

    def relay(n, t, df):
        arrive(n, t, "s%d+" % df, (df, -1), "all")
        push(n, t, "t%d+" % df, (df, -1), "lo")
        arrive(n, t, "s%d-" % df, (df, 1), "all")
        push(n, t, "t%d-" % df, (df, 1), "hi")

    def gather_stage(stage, n):
        if n_row == 1:
            return
        trees = (0, 1)
        if stage == 0:
            for t in trees:
                push(n, t, "f+", (0, 0), "all", True)
                push(n, t, "f-", (0, 0), "all", True)
            for t in trees:
                push(n, t, "s0+", (0, 0), "all", True)
                push(n, t, "s0-", (0, 0), "all", True)
        elif stage == 1:
            for t in trees:
                arrive(n, t, "f+", (-1, 0), "all")
                push(n, t, "g+", (-1, 0), "lo")
                arrive(n, t, "f-", (1, 0), "all")
                push(n, t, "g-", (1, 0), "hi")
            for t in trees:
                across(n, t, -1)
                across(n, t, 1)
        elif stage == 2:
            for t in trees:
                relay(n, t, 0)
        elif stage == 3:
            for t in trees:
                arrive(n, t, "g+", (2, 0), "lo")
                arrive(n, t, "g-", (2, 0), "hi")
                across(n, t, 2)
        elif stage == 4:
            for t in trees:
                relay(n, t, -1)
                relay(n, t, 1)
        elif stage == 5:
            for t in trees:
                relay(n, t, 2)
        elif stage == 6:
            for t in trees:
                for df in (0, -1, 1, 2):
                    arrive(n, t, "t%d+" % df, (df, 2), "lo")
                    arrive(n, t, "t%d-" % df, (df, 2), "hi")

    for n in range(PARTS):
        gather_stage(0, n)
    hello(0)
    emb_copy = pltpu.make_async_copy(emb_hbm, emb, emb_sem)
    emb_copy.start()
    for stage in (1, 2, 3, 4):
        for n in range(PARTS):
            gather_stage(stage, n)
        if stage == 3:
            hello_end(0)
            hello(1)
    gather_stage(5, 0)
    hello_end(1)
    hello(2)
    gather_stage(6, 0)

    emb_copy.wait()
    own_copy.wait()

    mm = min(1024, rows // 2)

    def lane_lse(vals):
        peak = tree_reduce(jnp.maximum, vals)
        return peak + jnp.log2(tree_reduce(jnp.add, [jnp.exp2(v - peak) for v in vals]))

    span_tiles = span // TILE

    def score_blocks(n, first, last):
        def block(i, carry):
            row0 = pl.multiple_of(i * mm, mm)
            acc = jnp.dot(
                emb[pl.ds(row0, mm), :],
                feat[:, n * span : (n + 1) * span],
                preferred_element_type=jnp.float32,
            )
            for a in range(mm // TILE):
                bias = [
                    jnp.where(mask_ref[n * span_tiles + j, i * (mm // TILE) + a] == 1, 0.0, NEGATIVE)
                    for j in range(span_tiles)
                ]
                for g in range(a * TILE, (a + 1) * TILE, 8):
                    vals = [
                        acc[g : g + 8, j * TILE : (j + 1) * TILE] * scale + bias[j]
                        for j in range(span_tiles)
                    ]
                    for j in range(span_tiles):
                        col0 = (n * span_tiles + j) * TILE
                        sim[pl.ds(row0 + g, 8), col0 : col0 + TILE] = vals[j]
                    if n > 0:
                        vals.append(wide[pl.ds(row0 + g, 8), :])
                    wide[pl.ds(row0 + g, 8), :] = lane_lse(vals)
            return carry

        lax.fori_loop(first, last, block, 0)

    blocks = rows // mm
    if PARTS > 1:
        score_blocks(0, 0, max(blocks // 4, 1))
        for n in range(1, PARTS):
            gather_stage(5, n)
        score_blocks(0, max(blocks // 4, 1), blocks)
        for n in range(1, PARTS):
            gather_stage(6, n)

    group = 64

    def lanes(shifts):
        return [jnp.broadcast_to(shifts[j : j + 1, :], (8, TILE)) for j in range(col_tiles)]

    half_rows, half_tiles = rows // 2, row_tiles // 2

    def row_partial(shifts, part):
        def block(step, carry):
            base = pl.multiple_of(step * group, group)
            for g in range(0, group, 8):
                wide[pl.ds(base + g, 8), :] = lane_lse(
                    [sim[pl.ds(base + g, 8), j * TILE : (j + 1) * TILE] + shifts[j] for j in range(col_tiles)]
                )
            return carry

        lax.fori_loop(part * half_rows // group, (part + 1) * half_rows // group, block, 0)

    def row_finish(k, part):
        def block(i, carry):
            t = jnp.transpose(wide[pl.ds(pl.multiple_of(i * TILE, TILE), TILE), :])
            peak = jnp.max(t, axis=0, keepdims=True)
            total = jnp.sum(jnp.exp2(t - peak), axis=0, keepdims=True)
            row_send[k, part, pl.ds(i - part * half_tiles, 1), :] = peak + jnp.log2(total)
            return carry

        lax.fori_loop(part * half_tiles, (part + 1) * half_tiles, block, 0, unroll=4)

    def exchange_start(send, recv, send_sem, recv_sem, at, n, target, near):
        for d in sorted(range(1, n), key=lambda d: (-near(d), d)):
            pltpu.make_async_remote_copy(
                src_ref=send.at[at],
                dst_ref=recv.at[at + (d - 1,)],
                send_sem=send_sem.at[at],
                recv_sem=recv_sem.at[at],
                device_id=target(d),
                device_id_type=MESH,
            ).start()

    def exchange_end(send, recv, send_sem, recv_sem, at, n, target):
        if n > 1:
            pltpu.make_async_remote_copy(
                src_ref=recv.at[at],
                dst_ref=recv.at[at],
                send_sem=send_sem.at[at],
                recv_sem=recv_sem.at[at],
                device_id=target(1),
                device_id_type=MESH,
            ).wait()
        parts = [send[at]] + [recv[at + (d - 1,)] for d in range(1, n)]
        peak = tree_reduce(jnp.maximum, parts)
        total = tree_reduce(jnp.add, [jnp.exp2(v - peak) for v in parts])
        return peak + jnp.log2(total)

    def spread_rows(part):
        def block(i, carry):
            u = jnp.broadcast_to(row_out[pl.ds(i, 1), :], (TILE, TILE))
            wide[pl.ds(pl.multiple_of(i * TILE, TILE), TILE), :] = jnp.transpose(u)
            return carry

        lax.fori_loop(part * half_tiles, (part + 1) * half_tiles, block, 0, unroll=4)

    def column_partial(part, start):
        def block(i, carry):
            base = pl.multiple_of(i * TILE, TILE)
            out = []
            for j in range(col_tiles):
                top, total = carry[j]
                v = sim[pl.ds(base, TILE), j * TILE : (j + 1) * TILE] + wide[pl.ds(base, TILE), :]
                v = v.reshape(TILE // 8, 8, TILE)
                new = jnp.maximum(top, tree_reduce(jnp.maximum, [v[g] for g in range(TILE // 8)]))
                add = tree_reduce(jnp.add, [jnp.exp2(v[g] - new) for g in range(TILE // 8)])
                out.append((new, total * jnp.exp2(top - new) + add))
            return tuple(out)

        return lax.fori_loop(part * half_tiles, (part + 1) * half_tiles, block, start)

    def column_finish(k, done):
        for j in range(col_tiles):
            level = done[j][0] + jnp.log2(done[j][1])
            peak = jnp.max(level, axis=0, keepdims=True)
            total = jnp.sum(jnp.exp2(level - peak), axis=0, keepdims=True)
            col_send[k, j : j + 1, :] = peak + jnp.log2(total)

    def proto_peer(d):
        return (r, lax.rem(p + d, n_proto))

    def row_peer(d):
        return (lax.rem(r + d, n_row), p)

    def wrap(d, n):
        return min(d, n - d)

    row_refs = (row_send, row_recv, rs_sem, rr_sem)
    col_refs = (col_send, col_recv, cs_sem, cr_sem)

    def row_near(d):
        return wrap(d, n_proto)

    def col_near(d):
        return wrap(d // side, side) + wrap(d % side, side)

    shifts = None
    for k in range(ITERS):
        for i in range(2):
            if k > 0:
                row_partial(shifts, i)
            else:
                for n in range(min(1, PARTS - 1), PARTS):
                    score_blocks(n, i * half_rows // mm, (i + 1) * half_rows // mm)
            row_finish(k, i)
            if (k, i) == (0, 0):
                hello_end(2)
            exchange_start(*row_refs, (k, i), n_proto, proto_peer, row_near)
        if k == 0:
            for i in range(0, protos, TILE):
                for j in range(0, depth, TILE):
                    feat_t[i : i + TILE, j : j + TILE] = jnp.transpose(feat[j : j + TILE, i : i + TILE])
        columns = tuple(
            (jnp.full((8, TILE), LOWEST, jnp.float32), jnp.zeros((8, TILE), jnp.float32))
            for _ in range(col_tiles)
        )
        for i in range(2):
            row_out[i * half_tiles : (i + 1) * half_tiles, :] = -exchange_end(
                *row_refs, (k, i), n_proto, proto_peer
            )
            spread_rows(i)
            columns = column_partial(i, columns)
        column_finish(k, columns)
        exchange_start(*col_refs, (k,), n_row, row_peer, col_near)
        potential = log_column - exchange_end(*col_refs, (k,), n_row, row_peer)
        shifts = lanes(potential)

    col_out[...] = potential * LN2

    plan = emb
    far = n_z // 2
    order = [far] + [t for d in range(far - 1, 0, -1) for t in (d, n_z - d)] + [0] if far else [0]
    pairs = [order[i : i + 2] for i in range(0, len(order), 2)]
    width = rows // SPLIT
    mp = rows // 2
    sent_sibling = []

    def plan_block(base):
        for g in range(0, mp, 16):
            shift = [wide[pl.ds(base + g + e, 8), :] for e in (0, 8)]
            for j in range(col_tiles):
                v = [
                    jnp.exp2(sim[pl.ds(base + g + e, 8), j * TILE : (j + 1) * TILE] + (shift[e // 8] + shifts[j]))
                    for e in (0, 8)
                ]
                plan[pl.ds(base + g, 16), j * TILE : (j + 1) * TILE] = jnp.concatenate(v, axis=0).astype(
                    jnp.bfloat16
                )

    def product(ts, base):
        weights = [
            feat_t[:, pl.ds(pl.multiple_of(lax.rem(z + t, n_z) * 2 * share, 2 * share), 2 * share)] for t in ts
        ]
        acc = jnp.dot(
            plan[pl.ds(base, mp), :],
            jnp.concatenate(weights, axis=1) if len(ts) > 1 else weights[0],
            preferred_element_type=jnp.float32,
        )
        for i, t in enumerate(ts):
            part[t, :, pl.ds(base, mp)] = jnp.transpose(acc[:, i * 2 * share : (i + 1) * 2 * share]).astype(
                jnp.bfloat16
            )

    def sibling_copy(t, h):
        other = 1 - c
        return pltpu.make_async_remote_copy(
            src_ref=part.at[t, pl.ds(pl.multiple_of(other * share, share), share), h * width : (h + 1) * width],
            dst_ref=sib_recv.at[t, h],
            send_sem=ss_sem.at[t, h],
            recv_sem=sr_sem.at[t, h],
            device_id=(r, z * 2 + other),
            device_id_type=MESH,
        )

    def to_sibling(ts, hs):
        for t in ts:
            for h in hs:
                copy = sibling_copy(t, h)
                copy.start()
                sent_sibling.append(copy)

    def chip_sum(t, h):
        sibling_copy(t, h).wait_recv()
        mine = part[t, pl.ds(pl.multiple_of(c * share, share), share), h * width : (h + 1) * width]
        return mine.astype(jnp.float32) + sib_recv[t, h].astype(jnp.float32)

    def chain_copy(way, d, h):
        step = 1 if way == 0 else n_z - 1
        return pltpu.make_async_remote_copy(
            src_ref=tx.at[way, d - 1, h],
            dst_ref=rx.at[way, d - 1, h],
            send_sem=ts_sem.at[way, d - 1, h],
            recv_sem=tr_sem.at[way, d - 1, h],
            device_id=(r, lax.rem(z + step, n_z) * 2 + c),
            device_id_type=MESH,
        )

    flying = []
    lower, upper = list(range(SPLIT // 2)), list(range(SPLIT // 2, SPLIT))
    whole_way = (lower, upper)
    rest = (upper, lower)

    def forward(way, d, hs):
        t = d if way == 0 else n_z - d
        for h in hs:
            value = chip_sum(t, h)
            if d < far and (d + 1 < far or h in whole_way[way]):
                chain_copy(way, d + 1, h).wait_recv()
                value = value + rx[way, d, h].astype(jnp.float32)
            tx[way, d - 1, h] = value.astype(jnp.bfloat16)
            copy = chain_copy(way, d, h)
            copy.start()
            flying.append(copy)

    def later_pair(n):
        if n < len(pairs):

            def block(i, carry):
                product(pairs[n], pl.multiple_of(i * mp, mp))
                return carry

            lax.fori_loop(0, 2, block, 0)
            to_sibling(pairs[n], lower + upper)

    for i, hs in enumerate((lower, upper)):
        plan_block(i * mp)
        product(pairs[0], i * mp)
        to_sibling(pairs[0], hs)
    if far:
        forward(0, far, lower)
        forward(1, far, upper)
    if far > 1:
        forward(0, far - 1, upper)
    later_pair(1)
    if far > 1:
        forward(1, far - 1, lower)
    later_pair(2)
    if far > 1:
        forward(0, far - 1, lower)
        forward(1, far - 1, upper)
    later_pair(3)
    for d in range(far - 2, 0, -1):
        for h, g in zip(upper + lower, lower + upper):
            forward(0, d, [h])
            forward(1, d, [g])
    for h in upper + lower:
        value = chip_sum(0, h)
        for way in (0, 1):
            if far > 1 or (far == 1 and h in whole_way[way]):
                chain_copy(way, 1, h).wait_recv()
                value = value + rx[way, 0, h].astype(jnp.float32)
        out_ref[:, h * width : (h + 1) * width] = value.astype(jnp.bfloat16)
    row_out[...] = row_out[...] * LN2

    for copy in sent + sent_sibling + flying:
        copy.wait_send()


def hand_over(a, b, c, a_out, b_out, c_out):
    a_out[...] = a[...]
    b_out[...] = b[...]
    c_out[...] = c[...]


def solution(mesh):
    n_row, n_proto = mesh.shape["row"], mesh.shape["proto"]
    side = math.isqrt(n_row)
    n_z = n_proto // 2
    far = max(n_z // 2, 1)

    def shards(embeddings, prototypes, block_mask):
        rows, depth = embeddings.shape
        protos, slab = prototypes.shape
        share = depth // n_proto
        row_tiles, col_tiles = rows // TILE, protos // TILE
        log_column = math.log2((rows * n_row) / (protos * n_proto))
        f32, bf16 = jnp.float32, jnp.bfloat16
        dma = pltpu.SemaphoreType.DMA
        peers_r, peers_p = max(n_row - 1, 1), max(n_proto - 1, 1)
        vmem = pl.BlockSpec(memory_space=pltpu.VMEM)
        shapes = (
            jax.ShapeDtypeStruct((share, rows), bf16),
            jax.ShapeDtypeStruct((row_tiles, TILE), f32),
            jax.ShapeDtypeStruct((col_tiles, TILE), f32),
        )
        results = pl.pallas_call(
            functools.partial(kernel, (side, n_row, n_proto, log_column)),
            out_shape=shapes,
            in_specs=[
                pl.BlockSpec(memory_space=pl.ANY),
                pl.BlockSpec(memory_space=pl.ANY),
                pl.BlockSpec(memory_space=pltpu.SMEM),
            ],
            out_specs=(vmem, vmem, vmem),
            scratch_shapes=[
                pltpu.VMEM((rows, depth), bf16),
                pltpu.VMEM((depth, protos), bf16),
                pltpu.VMEM((protos, depth), bf16),
                pltpu.VMEM((rows, protos), f32),
                pltpu.VMEM((rows, TILE), f32),
                pltpu.VMEM((ITERS, 2, row_tiles // 2, TILE), f32),
                pltpu.VMEM((ITERS, 2, peers_p, row_tiles // 2, TILE), f32),
                pltpu.VMEM((ITERS, col_tiles, TILE), f32),
                pltpu.VMEM((ITERS, peers_r, col_tiles, TILE), f32),
                pltpu.VMEM((n_z, 2 * share, rows), bf16),
                pltpu.VMEM((n_z, SPLIT, share, rows // SPLIT), bf16),
                pltpu.VMEM((2, far, SPLIT, share, rows // SPLIT), bf16),
                pltpu.VMEM((2, far, SPLIT, share, rows // SPLIT), bf16),
                dma(()),
                dma(()),
                dma((PARTS, 2, 20)),
                dma((PARTS, 2, 20)),
                dma((ITERS, 2)),
                dma((ITERS, 2)),
                dma((ITERS,)),
                dma((ITERS,)),
                dma((n_z, SPLIT)),
                dma((n_z, SPLIT)),
                dma((2, far, SPLIT)),
                dma((2, far, SPLIT)),
                pltpu.SemaphoreType.REGULAR((3,)),
            ],
            compiler_params=pltpu.CompilerParams(
                collective_id=0, has_side_effects=True, vmem_limit_bytes=56 * 1024 * 1024
            ),
        )(prototypes.T, embeddings, block_mask.T)
        targets, row_potential, column_potential = pl.pallas_call(hand_over, out_shape=shapes)(*results)
        return (
            targets.T,
            row_potential.reshape(rows),
            column_potential.reshape(protos),
        )

    return jax.shard_map(
        shards,
        mesh=mesh,
        in_specs=(P("row", None), P("proto", "row"), P("row", "proto")),
        out_specs=(P("row", "proto"), P("row"), P("proto")),
        check_vma=False,
    )
```
